256 devices in a mesh: space: 64 (over x, z, y_hi), batch: 4 (over y_lo, core).
Axes of the slice: x: 4, y: 4 (y_hi: 2, y_lo: 2; y = y_hi * 2 + y_lo), z: 8, core: 2. Of those that a mesh axis runs over, the one named last changes fastest.
Arguments:
- field: bfloat16 [4, 20, 128, 128, 512], P('batch', None, 'space'), may hold values from -6 to 6
- spectral_weight: bfloat16 [2, 24, 2304, 800], P(None, 'batch', 'space'), may hold values from -6 to 6
- local_weight: bfloat16 [2, 20, 20], replicated, may hold values from -1.25 to 1.25
- bias: float32 [2, 20], replicated, may hold values from -3 to 3
Outputs:
- next_field: bfloat16 [4, 20, 128, 128, 512], P('batch', None, 'space')
The draws below stay inside these ranges and needn't reach their ends.
All inputs are finite; a program needn't handle non-finite values.
Results may differ from the reference program's by a relative error of at most 0.02.
Values may be sent and summed in bfloat16 or wider, within the bound.
No kernel may reach another device: no remote copies, remote signals or barrier semaphores. Data moves between devices by JAX's collectives and lax.ppermute only.
A program may use at most 128 MiB of HBM per device.

```python
import math
import jax
import jax.numpy as jnp
from jax import lax

X = 128
Y = 128
VERTICAL_POINTS = 32
EPOCH_COUNT = 16
C = 20
MX = 24
MY = 24
MZ = 12
MT = 8
LAYERS = 2
SAMPLES = 4
MP = 2304


def levels(stream_key, extent, pieces, smallest, largest):
    gain, own = 1.0, jax.random.fold_in(stream_key, 6)
    for axis_at, blocks in pieces:
        heights = jnp.exp(jax.random.uniform(jax.random.fold_in(own, axis_at), (blocks,), jnp.float32, smallest / len(pieces), largest / len(pieces)))
        gain = gain * jnp.repeat(heights, extent[axis_at] // blocks).reshape([-1 if axis == axis_at else 1 for axis in range(len(extent))])
    return gain


def centred(key, extent, deviation, reach, split=(), held_as=jnp.bfloat16):
    result = jax.random.normal(key, extent, jnp.float32) * deviation
    if len(split) > 0:
        result = levels(key, extent, split, -0.22, 0.18) * result
    return jnp.clip(result, min=-reach, max=reach).astype(held_as)


def setup_inputs(seed: int = 0) -> dict:
    splits = jax.random.split(jax.random.key(seed), 5)
    field = centred(splits[0], (SAMPLES, C, X, Y, VERTICAL_POINTS * EPOCH_COUNT), 1.0, 6.0, ((0, 4), (2, 64)))
    spectral_weight = centred(splits[1], (LAYERS, MX, MP, 2 * C * C), 1.2, 6.0, ((1, 4), (2, 64)))
    local_weight = centred(splits[2], (LAYERS, C, C), C ** -0.5, 1.25)
    bias = centred(splits[3], (LAYERS, C), 0.5, 3.0, (), jnp.float32)
    return {"field": field, "spectral_weight": spectral_weight, "local_weight": local_weight, "bias": bias}


def line_tables(length, kept_count):
    half_count = kept_count // 2
    frequency = jnp.concatenate([jnp.arange(half_count, dtype=jnp.int32), jnp.arange(length - half_count, length, dtype=jnp.int32)])
    places = jnp.arange(length, dtype=jnp.int32)
    rotation_multipliers = places[:, None] * frequency[None, :] % length
    angles = 2.0 * math.pi / length * rotation_multipliers.astype(jnp.float32)
    norming = 1.0 / math.sqrt(length)
    cosine = jnp.cos(angles) * norming
    sine_part = jnp.sin(angles) * norming
    forward = jnp.stack([jnp.stack([cosine, -sine_part], 1), jnp.stack([sine_part, cosine], 1)], 1)
    inverse = jnp.stack([jnp.stack([cosine.T, sine_part.T], -1), jnp.stack([-sine_part.T, cosine.T], -1)], 1)
    return (forward.astype(jnp.bfloat16), inverse.astype(jnp.bfloat16))

def depth_tables():
    half_count = MZ // 2
    vertical_spatial_harmonic = jnp.concatenate([jnp.arange(half_count, dtype=jnp.int32), jnp.arange(VERTICAL_POINTS - half_count, VERTICAL_POINTS, dtype=jnp.int32)])
    clock_harmonic_index = jnp.arange(MT, dtype=jnp.int32)
    mesh_volumes = jnp.arange(VERTICAL_POINTS * EPOCH_COUNT, dtype=jnp.int32)
    vertical_coordinates = mesh_volumes // EPOCH_COUNT
    snapshot_moments = mesh_volumes % EPOCH_COUNT
    rotation_multipliers = (vertical_coordinates[:, None, None] * vertical_spatial_harmonic[None, :, None] * EPOCH_COUNT + snapshot_moments[:, None, None] * clock_harmonic_index[None, None, :] * VERTICAL_POINTS) % (VERTICAL_POINTS * EPOCH_COUNT)
    rotation_multipliers = rotation_multipliers.reshape(VERTICAL_POINTS * EPOCH_COUNT, MZ * MT)
    angles = 2.0 * math.pi / (VERTICAL_POINTS * EPOCH_COUNT) * rotation_multipliers.astype(jnp.float32)
    norming = 1.0 / math.sqrt(VERTICAL_POINTS * EPOCH_COUNT)
    cosine = jnp.cos(angles) * norming
    sine_part = jnp.sin(angles) * norming
    forward = jnp.concatenate([cosine, -sine_part], 1)
    doubling = jnp.where(clock_harmonic_index == 0, 1.0, 2.0).astype(jnp.float32)
    doubling = jnp.broadcast_to(doubling[None, :], (MZ, MT)).reshape(MZ * MT)
    inverse = jnp.concatenate([cosine.T * doubling[:, None], -sine_part.T * doubling[:, None]], 0)
    return (forward.astype(jnp.bfloat16), inverse.astype(jnp.bfloat16))

def reference(field, spectral_weight, local_weight, bias):
    forward_zt, inverse_zt = depth_tables()
    forward_y, inverse_y = line_tables(Y, MY)
    forward_x, inverse_x = line_tables(X, MX)
    modes_zt = MZ * MT
    pencil_count = MY * MZ * MT
    f32 = jnp.float32
    current = field
    for layer_index in range(LAYERS):
        weights = spectral_weight[layer_index].reshape(MX, pencil_count, 2, C, C).astype(f32)
        mixing = local_weight[layer_index].astype(f32)
        offset = bias[layer_index].astype(f32)

        def one_sample(sample):
            zt_modes = jnp.dot(sample.reshape(-1, VERTICAL_POINTS * EPOCH_COUNT), forward_zt, preferred_element_type=f32).astype(jnp.bfloat16)
            zt_modes = zt_modes.reshape(C * X, Y, 2, modes_zt)
            y_modes = jnp.einsum('nyrq,yrjm->njmq', zt_modes.astype(f32), forward_y.astype(f32)).astype(jnp.bfloat16)
            y_modes = y_modes.reshape(C, X, 2, pencil_count)
            x_modes = jnp.einsum('cxrp,xrjm->cjmp', y_modes.astype(f32), forward_x.astype(f32)).astype(jnp.bfloat16)
            real_in = x_modes[:, 0].astype(f32)
            imag_in = x_modes[:, 1].astype(f32)
            layout_shape = 'cmp,mpco->omp'
            real_out = jnp.einsum(layout_shape, real_in, weights[:, :, 0]) - jnp.einsum(layout_shape, imag_in, weights[:, :, 1])
            imag_out = jnp.einsum(layout_shape, real_in, weights[:, :, 1]) + jnp.einsum(layout_shape, imag_in, weights[:, :, 0])
            mixed = jnp.stack([real_out, imag_out], 1).astype(jnp.bfloat16)
            x_back = jnp.einsum('ojmp,mjxr->oxrp', mixed.astype(f32), inverse_x.astype(f32)).astype(jnp.bfloat16)
            x_back = x_back.reshape(C * X, 2, MY, modes_zt)
            y_back = jnp.einsum('njmq,mjyr->nyrq', x_back.astype(f32), inverse_y.astype(f32)).astype(jnp.bfloat16)
            y_back = y_back.reshape(C * X * Y, 2 * modes_zt)
            spectral = jnp.dot(y_back, inverse_zt, preferred_element_type=f32).reshape(C, X, Y, VERTICAL_POINTS * EPOCH_COUNT)
            local_term = jnp.einsum('cxyq,co->oxyq', sample.astype(f32), mixing)
            total = spectral + local_term + offset[:, None, None, None]
            return jax.nn.gelu(total, approximate=False).astype(jnp.bfloat16)
        current = lax.map(one_sample, current)
    return current
```

```python
import math

import jax
import jax.numpy as jnp
from jax import lax
from jax.sharding import PartitionSpec as P

X = 128
Y = 128
VERTICAL_POINTS = 32
EPOCH_COUNT = 16
C = 20
MX = 24
MY = 24
MZ = 12
MT = 8
LAYERS = 2


def line_tables(length, kept_count):
    half_count = kept_count // 2
    frequency = jnp.concatenate(
        [
            jnp.arange(half_count, dtype=jnp.int32),
            jnp.arange(length - half_count, length, dtype=jnp.int32),
        ]
    )
    places = jnp.arange(length, dtype=jnp.int32)
    rotation_multipliers = places[:, None] * frequency[None, :] % length
    angles = 2.0 * math.pi / length * rotation_multipliers.astype(jnp.float32)
    norming = 1.0 / math.sqrt(length)
    cosine = jnp.cos(angles) * norming
    sine_part = jnp.sin(angles) * norming
    forward = jnp.stack([jnp.stack([cosine, -sine_part], 1), jnp.stack([sine_part, cosine], 1)], 1)
    inverse = jnp.stack(
        [jnp.stack([cosine.T, sine_part.T], -1), jnp.stack([-sine_part.T, cosine.T], -1)], 1
    )
    return (forward.astype(jnp.bfloat16), inverse.astype(jnp.bfloat16))


def depth_tables():
    half_count = MZ // 2
    vertical_spatial_harmonic = jnp.concatenate(
        [
            jnp.arange(half_count, dtype=jnp.int32),
            jnp.arange(VERTICAL_POINTS - half_count, VERTICAL_POINTS, dtype=jnp.int32),
        ]
    )
    clock_harmonic_index = jnp.arange(MT, dtype=jnp.int32)
    mesh_volumes = jnp.arange(VERTICAL_POINTS * EPOCH_COUNT, dtype=jnp.int32)
    vertical_coordinates = mesh_volumes // EPOCH_COUNT
    snapshot_moments = mesh_volumes % EPOCH_COUNT
    rotation_multipliers = (
        vertical_coordinates[:, None, None] * vertical_spatial_harmonic[None, :, None] * EPOCH_COUNT
        + snapshot_moments[:, None, None] * clock_harmonic_index[None, None, :] * VERTICAL_POINTS
    ) % (VERTICAL_POINTS * EPOCH_COUNT)
    rotation_multipliers = rotation_multipliers.reshape(VERTICAL_POINTS * EPOCH_COUNT, MZ * MT)
    angles = (
        2.0 * math.pi / (VERTICAL_POINTS * EPOCH_COUNT) * rotation_multipliers.astype(jnp.float32)
    )
    norming = 1.0 / math.sqrt(VERTICAL_POINTS * EPOCH_COUNT)
    cosine = jnp.cos(angles) * norming
    sine_part = jnp.sin(angles) * norming
    forward = jnp.concatenate([cosine, -sine_part], 1)
    doubling = jnp.where(clock_harmonic_index == 0, 1.0, 2.0).astype(jnp.float32)
    doubling = jnp.broadcast_to(doubling[None, :], (MZ, MT)).reshape(MZ * MT)
    inverse = jnp.concatenate([cosine.T * doubling[:, None], -sine_part.T * doubling[:, None]], 0)
    return (forward.astype(jnp.bfloat16), inverse.astype(jnp.bfloat16))


def mix_block(modes, weights):
    freq_rows = weights.shape[0]
    pencils = weights.shape[1]
    split_weights = weights.reshape(freq_rows, pencils, 2, C, C)
    real_in = modes[:, :, 0]
    imag_in = modes[:, :, 1]
    layout_shape = "nhku,kuhw->nwku"
    real_out = jnp.einsum(
        layout_shape, real_in, split_weights[:, :, 0], preferred_element_type=jnp.float32
    ) - jnp.einsum(
        layout_shape, imag_in, split_weights[:, :, 1], preferred_element_type=jnp.float32
    )
    imag_out = jnp.einsum(
        layout_shape, real_in, split_weights[:, :, 1], preferred_element_type=jnp.float32
    ) + jnp.einsum(
        layout_shape, imag_in, split_weights[:, :, 0], preferred_element_type=jnp.float32
    )
    return jnp.stack([real_out, imag_out], 2).astype(jnp.bfloat16)


def body(field, spectral_weight, local_weight, bias):
    forward_zt, inverse_zt = depth_tables()
    forward_y, inverse_y = line_tables(Y, MY)
    forward_x, inverse_x = line_tables(X, MX)
    modes_zt = MZ * MT
    planes = field.shape[2]
    current = field
    weights = [
        lax.all_gather(spectral_weight[layer_index], "batch", axis=0, tiled=True)
        for layer_index in range(LAYERS)
    ]
    for layer_index in range(LAYERS):
        samples = current.shape[0]
        zt_modes = jnp.dot(
            current.reshape(-1, VERTICAL_POINTS * EPOCH_COUNT),
            forward_zt,
            preferred_element_type=jnp.float32,
        ).astype(jnp.bfloat16)
        zt_modes = zt_modes.reshape(samples * C * planes, Y, 2, modes_zt)
        y_modes = jnp.einsum(
            "nyrq,yrjm->njmq", zt_modes, forward_y, preferred_element_type=jnp.float32
        ).astype(jnp.bfloat16)
        y_modes = y_modes.reshape(samples, C, planes, 2, MY * modes_zt)
        x_modes = jnp.einsum(
            "scxrp,xrjm->scjmp",
            lax.all_to_all(y_modes, "space", split_axis=4, concat_axis=2, tiled=True),
            forward_x,
            preferred_element_type=jnp.float32,
        ).astype(jnp.bfloat16)
        mixed = mix_block(x_modes, weights[layer_index])
        x_back = jnp.einsum(
            "sojmp,mjxr->soxrp", mixed, inverse_x, preferred_element_type=jnp.float32
        ).astype(jnp.bfloat16)
        received = lax.all_to_all(x_back, "space", split_axis=2, concat_axis=4, tiled=True)
        item_count = received.shape[0]
        rows_view = received.reshape(item_count * C * planes, 2, MY, modes_zt)
        y_back = jnp.einsum(
            "njmq,mjyr->nyrq", rows_view, inverse_y, preferred_element_type=jnp.float32
        ).astype(jnp.bfloat16)
        flat_back = y_back.reshape(item_count * C * planes * Y, 2 * modes_zt)
        values = jnp.dot(flat_back, inverse_zt, preferred_element_type=jnp.float32)
        spectral = values.reshape(item_count, C, planes, Y, VERTICAL_POINTS * EPOCH_COUNT)
        local_term = jnp.einsum(
            "scxyq,co->soxyq",
            current,
            local_weight[layer_index],
            preferred_element_type=jnp.float32,
        )
        total = spectral + local_term + bias[layer_index][None, :, None, None, None]
        current = jax.nn.gelu(total, approximate=False).astype(jnp.bfloat16)
    return current


def solution(mesh):
    placed = (P("batch", None, "space", None, None), P(None, "batch", "space", None), P(), P())
    return jax.shard_map(
        body,
        mesh=mesh,
        in_specs=placed,
        out_specs=P("batch", None, "space", None, None),
        check_vma=False,
    )
```

```python
import math

import jax
import jax.numpy as jnp
import numpy as np
from jax import lax
from jax.experimental import pallas as pl
from jax.experimental.pallas import tpu as pltpu
from jax.sharding import PartitionSpec as P

X = 128
Y = 128
VERTICAL_POINTS = 32
EPOCH_COUNT = 16
ZT = VERTICAL_POINTS * EPOCH_COUNT
C = 20
MX = 24
MY = 24
MZ = 12
MT = 8
LAYERS = 2

QL = 12
QH = MZ * MT // QL
GROUPS = MY * QH
PARTS = 3
HALF = C // 2
LANES = 128
PLANES = 2
OWNERS = X // PLANES
KX_GROUPS = 4
KX_PER = MX // KX_GROUPS
ROWS = 2 * 2 * KX_PER
PAIRS = 2
STEPS = HALF // PAIRS
STRIP = 16

ERF_COEFFICIENTS = (
    7.97884216e-01,
    3.63342831e-02,
    -3.31296180e-05,
    -5.52402773e-05,
    3.96912621e-06,
    -1.33447465e-07,
    1.80564042e-09,
)
ERF_LIMIT = 31.36


def line_table(length, kept_count):
    half = kept_count // 2
    frequency = np.concatenate([np.arange(half), np.arange(length - half, length)])
    angles = 2.0 * math.pi / length * (np.arange(length)[:, None] * frequency[None, :] % length)
    cosine = np.cos(angles) / math.sqrt(length)
    sine = np.sin(angles) / math.sqrt(length)
    forward = np.stack([np.stack([cosine, -sine], 1), np.stack([sine, cosine], 1)], 1)
    inverse = np.stack([np.stack([cosine.T, sine.T], -1), np.stack([-sine.T, cosine.T], -1)], 1)
    return forward, inverse


def depth_table():
    half = MZ // 2
    vertical = np.concatenate([np.arange(half), np.arange(VERTICAL_POINTS - half, VERTICAL_POINTS)])
    clock = np.arange(MT)
    cells = np.arange(ZT)
    turns = (
        (cells // EPOCH_COUNT)[:, None, None] * vertical[None, :, None] * EPOCH_COUNT
        + (cells % EPOCH_COUNT)[:, None, None] * clock[None, None, :] * VERTICAL_POINTS
    ) % ZT
    angles = 2.0 * math.pi / ZT * turns.reshape(ZT, MZ * MT)
    cosine = np.cos(angles) / math.sqrt(ZT)
    sine = np.sin(angles) / math.sqrt(ZT)
    doubling = np.broadcast_to(np.where(clock == 0, 1.0, 2.0)[None, :], (MZ, MT)).reshape(-1)
    kept = MZ * MT
    forward = np.zeros((ZT, 2 * LANES))
    forward[:, :kept] = cosine
    forward[:, LANES : LANES + kept] = -sine
    inverse = np.zeros((2 * LANES, ZT))
    inverse[:kept] = cosine.T * doubling[:, None]
    inverse[LANES : LANES + kept] = -sine.T * doubling[:, None]
    return forward, inverse


def build_tables():
    zt_forward, zt_inverse = depth_table()
    y_forward, y_inverse = line_table(Y, MY)
    x_forward, x_inverse = line_table(X, MX)
    eye = np.eye(2)
    y_fwd = np.einsum("yrjm,ab,uv->maujbrvy", y_forward, eye, eye)
    y_fwd = y_fwd.reshape(MY * 8, 4 * PLANES * Y)
    y_inv = np.einsum("mryj,ab,uv->ajuymbvr", y_inverse, eye, eye)
    y_inv = y_inv.reshape(4 * PLANES * Y, MY * 8)
    x_split = x_forward.reshape(OWNERS, PLANES, 2, 2, KX_GROUPS, KX_PER)
    x_re, x_im = x_split[:, :, :, 0], x_split[:, :, :, 1]
    parts = np.stack([np.stack([x_re, -x_im]), np.stack([x_im, x_re])])
    x_fwd = np.einsum("stiurgm,ab->gsatmibur", parts, eye)
    x_fwd = x_fwd.reshape(KX_GROUPS * 2 * ROWS, OWNERS * 8)
    x_split = x_inverse.reshape(KX_GROUPS, KX_PER, 2, OWNERS, PLANES, 2)
    x_inv = np.einsum("gmsiuj,ab,c,t->iaujgsbctm", x_split, eye, np.ones(2), np.ones(2))
    x_inv = x_inv.reshape(OWNERS * 8, KX_GROUPS * 4 * ROWS)
    spread = np.zeros((LANES, HALF, LANES))
    for channel in range(HALF):
        for ql in range(QL):
            for out in range(HALF):
                spread[channel * QL + ql, channel, out * QL + ql] = 1.0
    spread = spread.reshape(LANES, HALF * LANES)
    tile = np.einsum("pa,qb,o->pqaob", np.eye(PARTS), np.eye(QL), np.ones(HALF))
    tile = tile.reshape(PARTS * QL, PARTS, HALF * QL)
    tile = np.pad(tile, ((0, 0), (0, 0), (0, LANES - HALF * QL))).reshape(PARTS * QL, -1)
    gather = np.einsum("ci,hu,ta,rs,o->chtrsaiuo", np.eye(HALF), eye, eye, eye, np.ones(HALF))
    gather = gather.reshape(HALF * 8, 2 * C * C)
    held = [zt_forward, zt_inverse, y_fwd, y_inv, x_fwd, x_inv, spread, tile, gather]
    names = ["zt_fwd", "zt_inv", "y_fwd", "y_inv", "x_fwd", "x_inv", "spread", "tile", "gather"]
    return {
        name: table.astype(np.float32).astype(jnp.bfloat16) for name, table in zip(names, held)
    }


def lane_index(shape):
    return lax.broadcasted_iota(jnp.int32, shape, len(shape) - 1)


def dot(left, right):
    return jnp.dot(left, right, preferred_element_type=jnp.float32)


def forward_step(step, block, zt_fwd, y_fwd, modes_ref):
    columns = []
    for pair in range(PAIRS):
        rows = []
        for half in range(2):
            z = dot(block(half, pair), zt_fwd).astype(jnp.bfloat16)
            rows += [z[:, :LANES], z[:, LANES:]]
        columns.append(jnp.concatenate(rows, 0))
    modes = dot(y_fwd, jnp.concatenate(columns, 1))
    lane = lane_index((MY * 8, LANES))
    for pair in range(PAIRS):
        channel = step * PAIRS + pair
        own = modes[:, pair * LANES : (pair + 1) * LANES]
        mask = (lane >= channel * QL) & (lane < channel * QL + QL)
        for qh in range(QH):
            shift = lax.rem((channel - qh) * QL + LANES, LANES)
            moved = pltpu.roll(own, shift, 1)
            kept = modes_ref[:, qh].reshape(MY * 8, LANES)
            modes_ref[:, qh] = jnp.where(mask, moved, kept).reshape(MY, 8, LANES)


def forward_kernel(field_ref, zt_ref, y_ref, out_ref, modes_ref):
    step = pl.program_id(0)

    @pl.when(step == 0)
    def _():
        modes_ref[...] = jnp.zeros_like(modes_ref)

    def block(half, pair):
        return field_ref[half, pair].reshape(PLANES * Y, ZT)

    forward_step(step, block, zt_ref[...], y_ref[...], modes_ref)

    @pl.when(step == STEPS - 1)
    def _():
        out_ref[...] = modes_ref[...].reshape(GROUPS * 8, LANES).astype(jnp.bfloat16)


def whole(shape):
    return pl.BlockSpec(shape, lambda *_: (0,) * len(shape), pipeline_mode=pl.Buffered(1))


def field_spec():
    return pl.BlockSpec((2, PAIRS, PLANES, Y, ZT), lambda s: (0, s, 0, 0, 0))


MESSAGE = (GROUPS * 8, LANES)
MODES = pltpu.VMEM((MY, QH, 8, LANES), jnp.float32)


def forward_call(field, tables):
    return pl.pallas_call(
        forward_kernel,
        grid=(STEPS,),
        in_specs=[field_spec(), whole(tables["zt_fwd"].shape), whole(tables["y_fwd"].shape)],
        out_specs=whole(MESSAGE),
        out_shape=jax.ShapeDtypeStruct(MESSAGE, jnp.bfloat16),
        scratch_shapes=[MODES],
        compiler_params=pltpu.CompilerParams(vmem_limit_bytes=48 << 20),
        name="forward_zt_y",
    )(field, tables["zt_fwd"], tables["y_fwd"])


def gelu(x):
    s = jnp.minimum(x * x, ERF_LIMIT)
    p = jnp.float32(ERF_COEFFICIENTS[-1])
    for coefficient in ERF_COEFFICIENTS[-2::-1]:
        p = p * s + jnp.float32(coefficient)
    h = 0.5 * x
    return h + h * jnp.tanh(x * p)


def inverse_step(step, modes_ref, local_ref, y_inv, zt_inv, out_ref):
    lane = lane_index((MY * 8, LANES))
    columns = []
    for pair in range(PAIRS):
        channel = step * PAIRS + pair
        value = jnp.zeros((MY * 8, LANES), jnp.float32)
        for qh in range(QH):
            shift = lax.rem((qh - channel) * QL + LANES, LANES)
            moved = pltpu.roll(modes_ref[:, qh].reshape(MY * 8, LANES), shift, 1)
            value = jnp.where((lane >= qh * QL) & (lane < qh * QL + QL), moved, value)
        columns.append(value.astype(jnp.bfloat16))
    back = dot(y_inv, jnp.concatenate(columns, 1)).astype(jnp.bfloat16)
    span = PLANES * Y
    for pair in range(PAIRS):
        own = back[:, pair * LANES : (pair + 1) * LANES]
        for half in range(2):
            at = 2 * half * span
            rows = jnp.concatenate([own[at : at + span], own[at + span : at + 2 * span]], 1)
            total = dot(rows, zt_inv) + local_ref[half, pair].reshape(span, ZT)
            out_ref[half, pair] = gelu(total).astype(jnp.bfloat16).reshape(PLANES, Y, ZT)


def load_modes(message_ref, modes_ref):
    modes_ref[...] = message_ref[...].astype(jnp.float32).reshape(MY, QH, 8, LANES)


def inverse_kernel(message_ref, local_ref, y_ref, zt_ref, out_ref, modes_ref):
    step = pl.program_id(0)

    @pl.when(step == 0)
    def _():
        load_modes(message_ref, modes_ref)

    inverse_step(step, modes_ref, local_ref, y_ref[...], zt_ref[...], out_ref)


FIELD = (2, HALF, PLANES, Y, ZT)


def inverse_call(message, local, tables):
    return pl.pallas_call(
        inverse_kernel,
        grid=(STEPS,),
        in_specs=[
            whole(MESSAGE),
            field_spec(),
            whole(tables["y_inv"].shape),
            whole(tables["zt_inv"].shape),
        ],
        out_specs=field_spec(),
        out_shape=jax.ShapeDtypeStruct(FIELD, jnp.bfloat16),
        scratch_shapes=[MODES],
        compiler_params=pltpu.CompilerParams(vmem_limit_bytes=48 << 20),
        name="inverse_zt_y",
    )(message, local, tables["y_inv"], tables["zt_inv"])


def mix_kernel(
    place_ref, message_ref, own, near, far, across, x_ref, inv_ref, spread_ref, out_ref, sums_ref
):
    span = OWNERS * 8
    message = message_ref[...].astype(jnp.float32).reshape(OWNERS, PARTS * 8, LANES)
    pieces = [
        message[:, part * 8 : part * 8 + 8].reshape(span, LANES).astype(jnp.bfloat16)
        for part in range(PARTS)
    ]
    group_rows = 2 * ROWS
    for distance, weights in enumerate((own, near, far, across)):
        group = place_ref[0] ^ distance
        table = x_ref[pl.ds(pl.multiple_of(group * group_rows, group_rows), group_rows), :]
        modes = dot(table, jnp.concatenate(pieces, 1)).astype(jnp.bfloat16)
        rows = [modes[:, part * LANES : (part + 1) * LANES] for part in range(PARTS)]
        spread = dot(jnp.concatenate(rows, 0), spread_ref[...])
        for part in range(PARTS):
            for out_half in range(2):
                totals = [None, None]
                for c10 in range(HALF):
                    at = ((c10 * PARTS + part) * 2 + out_half) * ROWS
                    weight = weights[at : at + ROWS, :].astype(jnp.float32)
                    for kind in range(2):
                        top = part * group_rows + kind * ROWS
                        term = spread[top : top + ROWS, c10 * LANES : (c10 + 1) * LANES] * weight
                        totals[kind] = term if c10 == 0 else totals[kind] + term
                for kind in range(2):
                    start = group * (4 * ROWS) + (kind * 2 + out_half) * ROWS
                    sums_ref[
                        pl.ds(pl.multiple_of(start, 8), ROWS), part * LANES : (part + 1) * LANES
                    ] = totals[kind]
    back = dot(inv_ref[...], sums_ref[...].astype(jnp.bfloat16))
    blocks = [
        back[:, part * LANES : (part + 1) * LANES].reshape(OWNERS, 8, LANES)
        for part in range(PARTS)
    ]
    out_ref[...] = jnp.concatenate(blocks, 1).reshape(GROUPS * 8, LANES).astype(jnp.bfloat16)


def mix_call(place, message, weights, tables):
    held = [tables["x_fwd"], tables["x_inv"], tables["spread"]]
    return pl.pallas_call(
        mix_kernel,
        grid=(1,),
        in_specs=[pl.BlockSpec(memory_space=pltpu.SMEM), whole(MESSAGE)]
        + [whole(w.shape) for w in weights]
        + [whole(t.shape) for t in held],
        out_specs=whole(MESSAGE),
        out_shape=jax.ShapeDtypeStruct(MESSAGE, jnp.bfloat16),
        scratch_shapes=[pltpu.VMEM((KX_GROUPS * 4 * ROWS, PARTS * LANES), jnp.float32)],
        compiler_params=pltpu.CompilerParams(vmem_limit_bytes=48 << 20),
        name="mix_x",
    )(place, message, *weights, *held)


def arrange_kernel(weight_ref, tile_ref, gather_ref, out_ref, rows_ref):
    kx = pl.program_id(0)
    tiled = lax.dot_general(
        weight_ref[0, 0],
        tile_ref[...],
        (((0,), (0,)), ((), ())),
        preferred_element_type=jnp.float32,
    )
    row = lax.broadcasted_iota(jnp.int32, tiled.shape, 0)
    place = lax.rem(lane_index(tiled.shape), LANES)
    first = lax.rem(row, HALF) * QL
    kept = jnp.where((place >= first) & (place < first + QL), tiled, 0.0)
    moved = dot(gather_ref[...], kept.astype(jnp.bfloat16))
    for c10 in range(HALF):
        for part in range(PARTS):
            start = (c10 * PARTS + part) * 2 * ROWS
            rows_ref[pl.ds(start + kx, 8, stride=KX_PER), :] = moved[
                c10 * 8 : c10 * 8 + 8, part * LANES : (part + 1) * LANES
            ]

    @pl.when(kx == KX_PER - 1)
    def _():
        out_ref[...] = rows_ref[...].astype(jnp.bfloat16)


def arrange_weights(weights, layer, tables):
    shape = (HALF * PARTS * 2 * ROWS, LANES)
    held = [tables["tile"], tables["gather"]]
    return pl.pallas_call(
        arrange_kernel,
        grid=(KX_PER,),
        in_specs=[pl.BlockSpec((1, 1) + weights.shape[2:], lambda k: (layer, k, 0, 0))]
        + [whole(t.shape) for t in held],
        out_specs=whole(shape),
        out_shape=jax.ShapeDtypeStruct(shape, jnp.bfloat16),
        scratch_shapes=[pltpu.VMEM(shape, jnp.float32)],
        compiler_params=pltpu.CompilerParams(vmem_limit_bytes=48 << 20),
        name="arrange_weights",
    )(weights, *held)


def swap(value, distance):
    return lax.ppermute(value, "batch", [(i, i ^ distance) for i in range(KX_GROUPS)])


def spread_weights(own):
    far = swap(own, 2)
    return own, swap(own, 1), far, swap(far, 1)


def exchange(message):
    grouped = message.reshape(OWNERS, PARTS * 8, LANES)
    moved = lax.all_to_all(grouped, "space", split_axis=0, concat_axis=0, tiled=True)
    return moved.reshape(MESSAGE)


def local_kernel(offset_ref, weight_ref, field_ref, out_ref, mixing_ref):
    size = C * STRIP

    @pl.when((pl.program_id(0) == 0) & (pl.program_id(1) == 0))
    def _():
        row = lax.broadcasted_iota(jnp.int32, (size, C), 0) // STRIP
        pick_out = (row == lane_index((size, C))).astype(jnp.bfloat16)
        lane = lane_index((C, size)) // STRIP
        pick_in = (lax.broadcasted_iota(jnp.int32, (C, size), 0) == lane).astype(jnp.bfloat16)
        rows = dot(pick_out, weight_ref[...]).astype(jnp.bfloat16)
        full = dot(rows, pick_in)
        same = lax.rem(lax.broadcasted_iota(jnp.int32, (size, size), 0), STRIP) == lax.rem(
            lane_index((size, size)), STRIP
        )
        mixing_ref[...] = jnp.where(same, full, 0.0).astype(jnp.bfloat16)

    mixed = dot(mixing_ref[...], field_ref[...].reshape(size, ZT))
    for half in range(2):
        for c10 in range(HALF):
            channel = half * HALF + c10
            rows = mixed[channel * STRIP : (channel + 1) * STRIP]
            out_ref[half, c10, 0] = rows + offset_ref[channel]


def local_term(current, weight, offset):
    spec = pl.BlockSpec((2, HALF, 1, STRIP, ZT), lambda p, y: (0, 0, p, y, 0))
    return pl.pallas_call(
        local_kernel,
        grid=(PLANES, Y // STRIP),
        in_specs=[pl.BlockSpec(memory_space=pltpu.SMEM), whole((C, C)), spec],
        out_specs=spec,
        out_shape=jax.ShapeDtypeStruct(FIELD, jnp.float32),
        scratch_shapes=[pltpu.VMEM((C * STRIP, C * STRIP), jnp.bfloat16)],
        compiler_params=pltpu.CompilerParams(vmem_limit_bytes=48 << 20),
        name="local_mixing",
    )(offset, weight.T, current)


def body(field, spectral_weight, local_weight, bias):
    tables = {name: jnp.asarray(table) for name, table in build_tables().items()}
    place = lax.axis_index("batch").astype(jnp.int32).reshape(1)
    current = field.reshape(FIELD)
    weights = None
    for layer in range(LAYERS):
        with jax.named_scope("forward"):
            message = forward_call(current, tables)
        if weights is None:
            message, spectral_weight = lax.optimization_barrier((message, spectral_weight))
            weights = [
                spread_weights(arrange_weights(spectral_weight, i, tables)) for i in range(LAYERS)
            ]
        received = exchange(message)
        with jax.named_scope("mix"):
            back = mix_call(place, received, weights[layer], tables)
        local = local_term(current, local_weight[layer], bias[layer])
        with jax.named_scope("inverse"):
            current = inverse_call(exchange(back), local, tables)
    return current.reshape(field.shape)


def solution(mesh):
    placed = (P("batch", None, "space", None, None), P(None, "batch", "space", None), P(), P())
    return jax.shard_map(
        body,
        mesh=mesh,
        in_specs=placed,
        out_specs=P("batch", None, "space", None, None),
        check_vma=False,
    )
```

```python
import math

import jax
import jax.numpy as jnp
import numpy as np
from jax import lax
from jax.experimental import pallas as pl
from jax.experimental.pallas import tpu as pltpu
from jax.sharding import PartitionSpec as P

X = 128
Y = 128
VERTICAL_POINTS = 32
EPOCH_COUNT = 16
ZT = VERTICAL_POINTS * EPOCH_COUNT
C = 20
MX = 24
MY = 24
MZ = 12
MT = 8
LAYERS = 2

QL = 12
QH = MZ * MT // QL
GROUPS = MY * QH
PARTS = 3
HALF = C // 2
LANES = 128
PLANES = 2
OWNERS = X // PLANES
KX_GROUPS = 4
KX_PER = MX // KX_GROUPS
ROWS = 2 * 2 * KX_PER
PAIRS = 2
STEPS = HALF // PAIRS
STRIP = 16
LOCAL_ROWS = 64
VMEM_BYTES = 58 << 20

ERF_COEFFICIENTS = (
    7.97884216e-01,
    3.63342831e-02,
    -3.31296180e-05,
    -5.52402773e-05,
    3.96912621e-06,
    -1.33447465e-07,
    1.80564042e-09,
)
ERF_LIMIT = 31.36


def line_table(length, kept_count):
    half = kept_count // 2
    frequency = np.concatenate([np.arange(half), np.arange(length - half, length)])
    angles = 2.0 * math.pi / length * (np.arange(length)[:, None] * frequency[None, :] % length)
    cosine = np.cos(angles) / math.sqrt(length)
    sine = np.sin(angles) / math.sqrt(length)
    forward = np.stack([np.stack([cosine, -sine], 1), np.stack([sine, cosine], 1)], 1)
    inverse = np.stack([np.stack([cosine.T, sine.T], -1), np.stack([-sine.T, cosine.T], -1)], 1)
    return forward, inverse


def depth_table():
    half = MZ // 2
    vertical = np.concatenate([np.arange(half), np.arange(VERTICAL_POINTS - half, VERTICAL_POINTS)])
    clock = np.arange(MT)
    cells = np.arange(ZT)
    turns = (
        (cells // EPOCH_COUNT)[:, None, None] * vertical[None, :, None] * EPOCH_COUNT
        + (cells % EPOCH_COUNT)[:, None, None] * clock[None, None, :] * VERTICAL_POINTS
    ) % ZT
    angles = 2.0 * math.pi / ZT * turns.reshape(ZT, MZ * MT)
    cosine = np.cos(angles) / math.sqrt(ZT)
    sine = np.sin(angles) / math.sqrt(ZT)
    doubling = np.broadcast_to(np.where(clock == 0, 1.0, 2.0)[None, :], (MZ, MT)).reshape(-1)
    kept = MZ * MT
    forward = np.zeros((ZT, 2 * LANES))
    forward[:, :kept] = cosine
    forward[:, LANES : LANES + kept] = -sine
    inverse = np.zeros((2 * LANES, ZT))
    inverse[:kept] = cosine.T * doubling[:, None]
    inverse[LANES : LANES + kept] = -sine.T * doubling[:, None]
    return forward, inverse


def build_tables():
    zt_forward, zt_inverse = depth_table()
    y_forward, y_inverse = line_table(Y, MY)
    x_forward, x_inverse = line_table(X, MX)
    eye = np.eye(2)
    y_fwd = np.einsum("yrjm,ab,uv->maujbrvy", y_forward, eye, eye)
    y_fwd = y_fwd.reshape(MY * 8, 4 * PLANES * Y)
    y_inv = np.einsum("mryj,ab,uv->ajuymbvr", y_inverse, eye, eye)
    y_inv = y_inv.reshape(4 * PLANES * Y, MY * 8)
    x_split = x_forward.reshape(OWNERS, PLANES, 2, 2, KX_GROUPS, KX_PER)
    x_re, x_im = x_split[:, :, :, 0], x_split[:, :, :, 1]
    parts = np.stack([np.stack([x_re, -x_im]), np.stack([x_im, x_re])])
    x_fwd = np.einsum("stiurgm,ab->gsatmibur", parts, eye)
    x_fwd = x_fwd.reshape(KX_GROUPS * 2 * ROWS, OWNERS * 8)
    x_split = x_inverse.reshape(KX_GROUPS, KX_PER, 2, OWNERS, PLANES, 2)
    x_inv = np.einsum("gmsiuj,ab,c,t->iaujgsbctm", x_split, eye, np.ones(2), np.ones(2))
    x_inv = x_inv.reshape(OWNERS * 8, KX_GROUPS * 4 * ROWS)
    spread = np.zeros((LANES, HALF, LANES))
    for channel in range(HALF):
        for ql in range(QL):
            for out in range(HALF):
                spread[channel * QL + ql, channel, out * QL + ql] = 1.0
    spread = spread.reshape(LANES, HALF * LANES)
    tile = np.einsum("pa,qb,o->pqaob", np.eye(PARTS), np.eye(QL), np.ones(HALF))
    tile = tile.reshape(PARTS * QL, PARTS, HALF * QL)
    tile = np.pad(tile, ((0, 0), (0, 0), (0, LANES - HALF * QL))).reshape(PARTS * QL, -1)
    gather = np.einsum("ci,hu,ta,rs,o->chtrsaiuo", np.eye(HALF), eye, eye, eye, np.ones(HALF))
    gather = gather.reshape(HALF * 8, 2 * C * C)
    mask = np.zeros((2 * C * C, LANES))
    for row in range(2 * C * C):
        mask[row, row % HALF * QL : (row % HALF + 1) * QL] = 1.0
    held = {
        "zt_fwd": zt_forward,
        "zt_inv": zt_inverse,
        "y_fwd": y_fwd,
        "y_inv": y_inv,
        "x_fwd": x_fwd,
        "x_inv": x_inv,
        "spread": spread,
        "tile": tile,
        "mask": mask,
        "gather": gather,
    }
    return {name: table.astype(np.float32).astype(jnp.bfloat16) for name, table in held.items()}


def lane_index(shape):
    return lax.broadcasted_iota(jnp.int32, shape, len(shape) - 1)


def dot(left, right):
    return jnp.dot(left, right, preferred_element_type=jnp.float32)


def forward_step(step, block, zt_fwd, y_fwd, modes_ref):
    columns = []
    for pair in range(PAIRS):
        rows = []
        for half in range(2):
            z = dot(block(half, pair), zt_fwd).astype(jnp.bfloat16)
            rows += [z[:, :LANES], z[:, LANES:]]
        columns.append(jnp.concatenate(rows, 0))
    modes = dot(y_fwd, jnp.concatenate(columns, 1))
    lane = lane_index((MY * 8, LANES))
    for pair in range(PAIRS):
        channel = step * PAIRS + pair
        own = modes[:, pair * LANES : (pair + 1) * LANES]
        mask = (lane >= channel * QL) & (lane < channel * QL + QL)
        for qh in range(QH):
            shift = lax.rem((channel - qh) * QL + LANES, LANES)
            moved = pltpu.roll(own, shift, 1)
            kept = modes_ref[:, qh].reshape(MY * 8, LANES)
            modes_ref[:, qh] = jnp.where(mask, moved, kept).reshape(MY, 8, LANES)


def forward_kernel(field_ref, zt_ref, y_ref, out_ref, modes_ref):
    step = pl.program_id(0)

    @pl.when(step == 0)
    def _():
        modes_ref[...] = jnp.zeros_like(modes_ref)

    def block(half, pair):
        return field_ref[half, pair].reshape(PLANES * Y, ZT)

    forward_step(step, block, zt_ref[...], y_ref[...], modes_ref)

    @pl.when(step == STEPS - 1)
    def _():
        out_ref[...] = modes_ref[...].reshape(GROUPS * 8, LANES).astype(jnp.bfloat16)


def whole(shape):
    return pl.BlockSpec(shape, lambda *_: (0,) * len(shape), pipeline_mode=pl.Buffered(1))


def field_spec():
    return pl.BlockSpec((2, PAIRS, PLANES, Y, ZT), lambda s: (0, s, 0, 0, 0))


MESSAGE = (GROUPS * 8, LANES)
MODES = pltpu.VMEM((MY, QH, 8, LANES), jnp.float32)


def forward_call(field, tables):
    return pl.pallas_call(
        forward_kernel,
        grid=(STEPS,),
        in_specs=[field_spec(), whole(tables["zt_fwd"].shape), whole(tables["y_fwd"].shape)],
        out_specs=whole(MESSAGE),
        out_shape=jax.ShapeDtypeStruct(MESSAGE, jnp.bfloat16),
        scratch_shapes=[MODES],
        compiler_params=pltpu.CompilerParams(vmem_limit_bytes=VMEM_BYTES),
        name="forward_zt_y",
    )(field, tables["zt_fwd"], tables["y_fwd"])


def gelu(x):
    s = jnp.minimum(x * x, ERF_LIMIT)
    p = jnp.float32(ERF_COEFFICIENTS[-1])
    for coefficient in ERF_COEFFICIENTS[-2::-1]:
        p = p * s + jnp.float32(coefficient)
    h = 0.5 * x
    return h + h * jnp.tanh(x * p)


def inverse_step(step, modes_ref, local_ref, y_inv, zt_inv, out_ref):
    lane = lane_index((MY * 8, LANES))
    columns = []
    for pair in range(PAIRS):
        channel = step * PAIRS + pair
        value = jnp.zeros((MY * 8, LANES), jnp.float32)
        for qh in range(QH):
            shift = lax.rem((qh - channel) * QL + LANES, LANES)
            moved = pltpu.roll(modes_ref[:, qh].reshape(MY * 8, LANES), shift, 1)
            value = jnp.where((lane >= qh * QL) & (lane < qh * QL + QL), moved, value)
        columns.append(value.astype(jnp.bfloat16))
    back = dot(y_inv, jnp.concatenate(columns, 1)).astype(jnp.bfloat16)
    span = PLANES * Y
    results = {}
    for pair in range(PAIRS):
        own = back[:, pair * LANES : (pair + 1) * LANES]
        for half in range(2):
            at = 2 * half * span
            rows = jnp.concatenate([own[at : at + span], own[at + span : at + 2 * span]], 1)
            total = dot(rows, zt_inv) + local_ref[half, pair].reshape(span, ZT)
            result = gelu(total).astype(jnp.bfloat16)
            out_ref[half, pair] = result.reshape(PLANES, Y, ZT)
            results[half, pair] = result
    return results


def load_modes(message_ref, modes_ref):
    modes_ref[...] = message_ref[...].astype(jnp.float32).reshape(MY, QH, 8, LANES)


def inverse_kernel(message_ref, local_ref, y_ref, zt_ref, out_ref, modes_ref):
    step = pl.program_id(0)

    @pl.when(step == 0)
    def _():
        load_modes(message_ref, modes_ref)

    inverse_step(step, modes_ref, local_ref, y_ref[...], zt_ref[...], out_ref)


FIELD = (2, HALF, PLANES, Y, ZT)


def inverse_call(message, local, tables):
    return pl.pallas_call(
        inverse_kernel,
        grid=(STEPS,),
        in_specs=[
            whole(MESSAGE),
            field_spec(),
            whole(tables["y_inv"].shape),
            whole(tables["zt_inv"].shape),
        ],
        out_specs=field_spec(),
        out_shape=jax.ShapeDtypeStruct(FIELD, jnp.bfloat16),
        scratch_shapes=[MODES],
        compiler_params=pltpu.CompilerParams(vmem_limit_bytes=VMEM_BYTES),
        name="inverse_zt_y",
    )(message, local, tables["y_inv"], tables["zt_inv"])


def turn_kernel(
    message_ref,
    local_ref,
    y_inv_ref,
    zt_inv_ref,
    zt_ref,
    y_ref,
    out_ref,
    send_ref,
    modes_ref,
    next_ref,
):
    step = pl.program_id(0)

    @pl.when(step == 0)
    def _():
        load_modes(message_ref, modes_ref)
        next_ref[...] = jnp.zeros_like(next_ref)

    results = inverse_step(step, modes_ref, local_ref, y_inv_ref[...], zt_inv_ref[...], out_ref)
    forward_step(
        step, lambda half, pair: results[half, pair], zt_ref[...], y_ref[...], next_ref
    )

    @pl.when(step == STEPS - 1)
    def _():
        send_ref[...] = next_ref[...].reshape(GROUPS * 8, LANES).astype(jnp.bfloat16)


def turn_call(message, local, tables):
    held = [tables[name] for name in ("y_inv", "zt_inv", "zt_fwd", "y_fwd")]
    return pl.pallas_call(
        turn_kernel,
        grid=(STEPS,),
        in_specs=[whole(MESSAGE), field_spec()] + [whole(t.shape) for t in held],
        out_specs=[field_spec(), whole(MESSAGE)],
        out_shape=[
            jax.ShapeDtypeStruct(FIELD, jnp.bfloat16),
            jax.ShapeDtypeStruct(MESSAGE, jnp.bfloat16),
        ],
        scratch_shapes=[MODES, MODES],
        compiler_params=pltpu.CompilerParams(vmem_limit_bytes=VMEM_BYTES),
        name="inverse_then_forward",
    )(message, local, *held)


def mix_kernel(
    place_ref, message_ref, own, near, far, across, x_ref, inv_ref, spread_ref, out_ref, sums_ref
):
    span = OWNERS * 8
    message = message_ref[...].astype(jnp.float32).reshape(OWNERS, PARTS * 8, LANES)
    pieces = [
        message[:, part * 8 : part * 8 + 8].reshape(span, LANES).astype(jnp.bfloat16)
        for part in range(PARTS)
    ]
    group_rows = 2 * ROWS
    for distance, weights in enumerate((own, near, far, across)):
        group = place_ref[0] ^ distance
        table = x_ref[pl.ds(pl.multiple_of(group * group_rows, group_rows), group_rows), :]
        modes = dot(table, jnp.concatenate(pieces, 1)).astype(jnp.bfloat16)
        rows = [modes[:, part * LANES : (part + 1) * LANES] for part in range(PARTS)]
        spread = dot(jnp.concatenate(rows, 0), spread_ref[...])
        for part in range(PARTS):
            for out_half in range(2):
                totals = [None, None]
                for c10 in range(HALF):
                    at = ((c10 * PARTS + part) * 2 + out_half) * ROWS
                    weight = weights[at : at + ROWS, :].astype(jnp.float32)
                    for kind in range(2):
                        top = part * group_rows + kind * ROWS
                        term = spread[top : top + ROWS, c10 * LANES : (c10 + 1) * LANES] * weight
                        totals[kind] = term if c10 == 0 else totals[kind] + term
                for kind in range(2):
                    start = group * (4 * ROWS) + (kind * 2 + out_half) * ROWS
                    sums_ref[
                        pl.ds(pl.multiple_of(start, 8), ROWS), part * LANES : (part + 1) * LANES
                    ] = totals[kind]
    back = dot(inv_ref[...], sums_ref[...].astype(jnp.bfloat16))
    blocks = [
        back[:, part * LANES : (part + 1) * LANES].reshape(OWNERS, 8, LANES)
        for part in range(PARTS)
    ]
    out_ref[...] = jnp.concatenate(blocks, 1).reshape(GROUPS * 8, LANES).astype(jnp.bfloat16)


def mix_call(place, message, weights, tables):
    held = [tables["x_fwd"], tables["x_inv"], tables["spread"]]
    return pl.pallas_call(
        mix_kernel,
        grid=(1,),
        in_specs=[pl.BlockSpec(memory_space=pltpu.SMEM), whole(MESSAGE)]
        + [whole(w.shape) for w in weights]
        + [whole(t.shape) for t in held],
        out_specs=whole(MESSAGE),
        out_shape=jax.ShapeDtypeStruct(MESSAGE, jnp.bfloat16),
        scratch_shapes=[pltpu.VMEM((KX_GROUPS * 4 * ROWS, PARTS * LANES), jnp.float32)],
        compiler_params=pltpu.CompilerParams(vmem_limit_bytes=VMEM_BYTES),
        name="mix_x",
    )(place, message, *weights, *held)


def arrange_kernel(weight_ref, tile_ref, mask_ref, gather_ref, out_ref, rows_ref):
    own = mask_ref[...]
    for kx in range(KX_PER):
        tiled = lax.dot_general(
            weight_ref[0, kx],
            tile_ref[...],
            (((0,), (0,)), ((), ())),
            preferred_element_type=jnp.float32,
        )
        kept = [
            tiled[:, part * LANES : (part + 1) * LANES].astype(jnp.bfloat16) * own
            for part in range(PARTS)
        ]
        moved = dot(gather_ref[...], jnp.concatenate(kept, 1))
        for c10 in range(HALF):
            for part in range(PARTS):
                start = (c10 * PARTS + part) * 2 * ROWS
                rows_ref[pl.ds(start + kx, 8, stride=KX_PER), :] = moved[
                    c10 * 8 : c10 * 8 + 8, part * LANES : (part + 1) * LANES
                ]
    out_ref[...] = rows_ref[...].astype(jnp.bfloat16)


def arrange_weights(weights, layer, tables):
    shape = (HALF * PARTS * 2 * ROWS, LANES)
    held = [tables["tile"], tables["mask"], tables["gather"]]
    return pl.pallas_call(
        arrange_kernel,
        grid=(1,),
        in_specs=[pl.BlockSpec((1,) + weights.shape[1:], lambda k: (layer, 0, 0, 0))]
        + [whole(t.shape) for t in held],
        out_specs=whole(shape),
        out_shape=jax.ShapeDtypeStruct(shape, jnp.bfloat16),
        scratch_shapes=[pltpu.VMEM(shape, jnp.float32)],
        compiler_params=pltpu.CompilerParams(vmem_limit_bytes=VMEM_BYTES),
        name="arrange_weights",
    )(weights, *held)


def swap(value, distance):
    return lax.ppermute(value, "batch", [(i, i ^ distance) for i in range(KX_GROUPS)])


def spread_weights(own):
    far = swap(own, 2)
    return own, swap(own, 1), far, swap(far, 1)


def exchange(message):
    grouped = message.reshape(OWNERS, PARTS * 8, LANES)
    moved = lax.all_to_all(grouped, "space", split_axis=0, concat_axis=0, tiled=True)
    return moved.reshape(MESSAGE)


def local_kernel(offset_ref, weight_ref, field_ref, out_ref, mixing_ref):
    size = C * STRIP

    @pl.when((pl.program_id(0) == 0) & (pl.program_id(1) == 0))
    def _():
        row = lax.broadcasted_iota(jnp.int32, (size, C), 0) // STRIP
        pick_out = (row == lane_index((size, C))).astype(jnp.bfloat16)
        lane = lane_index((C, size)) // STRIP
        pick_in = (lax.broadcasted_iota(jnp.int32, (C, size), 0) == lane).astype(jnp.bfloat16)
        rows = dot(pick_out, weight_ref[...]).astype(jnp.bfloat16)
        full = dot(rows, pick_in)
        same = lax.rem(lax.broadcasted_iota(jnp.int32, (size, size), 0), STRIP) == lax.rem(
            lane_index((size, size)), STRIP
        )
        mixing_ref[...] = jnp.where(same, full, 0.0).astype(jnp.bfloat16)

    for first in range(0, LOCAL_ROWS, STRIP):
        mixed = dot(mixing_ref[...], field_ref[:, :, 0, first : first + STRIP].reshape(size, ZT))
        for half in range(2):
            for c10 in range(HALF):
                channel = half * HALF + c10
                rows = mixed[channel * STRIP : (channel + 1) * STRIP] + offset_ref[channel]
                out_ref[half, c10, 0, first : first + STRIP] = rows.astype(jnp.bfloat16)


def local_term(current, weight, offset):
    spec = pl.BlockSpec((2, HALF, 1, LOCAL_ROWS, ZT), lambda p, y: (0, 0, p, y, 0))
    return pl.pallas_call(
        local_kernel,
        grid=(PLANES, Y // LOCAL_ROWS),
        in_specs=[pl.BlockSpec(memory_space=pltpu.SMEM), whole((C, C)), spec],
        out_specs=spec,
        out_shape=jax.ShapeDtypeStruct(FIELD, jnp.bfloat16),
        scratch_shapes=[pltpu.VMEM((C * STRIP, C * STRIP), jnp.bfloat16)],
        compiler_params=pltpu.CompilerParams(vmem_limit_bytes=VMEM_BYTES),
        name="local_mixing",
    )(offset, weight.T, current)


def after(value, *others):
    return lax.optimization_barrier((value,) + others)[0]


def body(field, spectral_weight, local_weight, bias):
    tables = {name: jnp.asarray(table) for name, table in build_tables().items()}
    place = lax.axis_index("batch").astype(jnp.int32).reshape(1)
    field = field.reshape(FIELD)
    own = arrange_weights(spectral_weight, 0, tables)
    weights = spread_weights(own)
    message = forward_call(field, dict(tables, zt_fwd=after(tables["zt_fwd"], own)))
    local = local_term(field, after(local_weight[0], message), bias[0])
    received = after(exchange(message), local)
    back = mix_call(place, received, weights, tables)
    own = arrange_weights(after(spectral_weight, back), 1, tables)
    weights = spread_weights(own)
    current, message = turn_call(after(exchange(back), own), local, tables)
    local = local_term(current, local_weight[1], bias[1])
    received = after(exchange(message), local)
    back = mix_call(place, received, weights, tables)
    return inverse_call(exchange(back), local, tables).reshape(1, C, PLANES, Y, ZT)


def solution(mesh):
    placed = (P("batch", None, "space", None, None), P(None, "batch", "space", None), P(), P())
    return jax.shard_map(
        body,
        mesh=mesh,
        in_specs=placed,
        out_specs=P("batch", None, "space", None, None),
        check_vma=False,
    )
```

```python
import math

import jax
import jax.numpy as jnp
import numpy as np
from jax import lax
from jax.experimental import pallas as pl
from jax.experimental.pallas import tpu as pltpu
from jax.sharding import PartitionSpec as P

X = 128
Y = 128
VERTICAL_POINTS = 32
EPOCH_COUNT = 16
ZT = VERTICAL_POINTS * EPOCH_COUNT
C = 20
MX = 24
MY = 24
MZ = 12
MT = 8
LAYERS = 2

QL = 12
QH = MZ * MT // QL
GROUPS = MY * QH
PARTS = 3
HALF = C // 2
LANES = 128
PLANES = 2
OWNERS = X // PLANES
KX_GROUPS = 4
KX_PER = MX // KX_GROUPS
ROWS = 2 * 2 * KX_PER
PAIRS = 2
STEPS = HALF // PAIRS
STRIP = 16
LOCAL_ROWS = 64
VMEM_BYTES = 48 << 20

ERF_COEFFICIENTS = (
    7.97884216e-01,
    3.63342831e-02,
    -3.31296180e-05,
    -5.52402773e-05,
    3.96912621e-06,
    -1.33447465e-07,
    1.80564042e-09,
)
ERF_LIMIT = 31.36


def line_table(length, kept_count):
    half = kept_count // 2
    frequency = np.concatenate([np.arange(half), np.arange(length - half, length)])
    angles = 2.0 * math.pi / length * (np.arange(length)[:, None] * frequency[None, :] % length)
    cosine = np.cos(angles) / math.sqrt(length)
    sine = np.sin(angles) / math.sqrt(length)
    forward = np.stack([np.stack([cosine, -sine], 1), np.stack([sine, cosine], 1)], 1)
    inverse = np.stack([np.stack([cosine.T, sine.T], -1), np.stack([-sine.T, cosine.T], -1)], 1)
    return forward, inverse


def depth_table():
    half = MZ // 2
    vertical = np.concatenate([np.arange(half), np.arange(VERTICAL_POINTS - half, VERTICAL_POINTS)])
    clock = np.arange(MT)
    cells = np.arange(ZT)
    turns = (
        (cells // EPOCH_COUNT)[:, None, None] * vertical[None, :, None] * EPOCH_COUNT
        + (cells % EPOCH_COUNT)[:, None, None] * clock[None, None, :] * VERTICAL_POINTS
    ) % ZT
    angles = 2.0 * math.pi / ZT * turns.reshape(ZT, MZ * MT)
    cosine = np.cos(angles) / math.sqrt(ZT)
    sine = np.sin(angles) / math.sqrt(ZT)
    doubling = np.broadcast_to(np.where(clock == 0, 1.0, 2.0)[None, :], (MZ, MT)).reshape(-1)
    kept = MZ * MT
    forward = np.zeros((ZT, 2 * LANES))
    forward[:, :kept] = cosine
    forward[:, LANES : LANES + kept] = -sine
    inverse = np.zeros((2 * LANES, ZT))
    inverse[:kept] = cosine.T * doubling[:, None]
    inverse[LANES : LANES + kept] = -sine.T * doubling[:, None]
    return forward, inverse


def build_tables():
    zt_forward, zt_inverse = depth_table()
    y_forward, y_inverse = line_table(Y, MY)
    x_forward, x_inverse = line_table(X, MX)
    eye = np.eye(2)
    y_fwd = np.einsum("yrjm,ab,uv->maujbrvy", y_forward, eye, eye)
    y_fwd = y_fwd.reshape(MY * 8, 4 * PLANES * Y)
    y_inv = np.einsum("mryj,ab,uv->ajuymbvr", y_inverse, eye, eye)
    y_inv = y_inv.reshape(4 * PLANES * Y, MY * 8)
    x_split = x_forward.reshape(OWNERS, PLANES, 2, 2, KX_GROUPS, KX_PER)
    x_re, x_im = x_split[:, :, :, 0], x_split[:, :, :, 1]
    parts = np.stack([np.stack([x_re, -x_im]), np.stack([x_im, x_re])])
    x_fwd = np.einsum("stiurgm,ab->gsatmibur", parts, eye)
    x_fwd = x_fwd.reshape(KX_GROUPS * 2 * ROWS, OWNERS * 8)
    x_split = x_inverse.reshape(KX_GROUPS, KX_PER, 2, OWNERS, PLANES, 2)
    x_inv = np.einsum("gmsiuj,ab,c,t->iaujgsbctm", x_split, eye, np.ones(2), np.ones(2))
    x_inv = x_inv.reshape(OWNERS * 8, KX_GROUPS * 4 * ROWS)
    spread = np.zeros((LANES, HALF, LANES))
    for channel in range(HALF):
        for ql in range(QL):
            for out in range(HALF):
                spread[channel * QL + ql, channel, out * QL + ql] = 1.0
    spread = spread.reshape(LANES, HALF * LANES)
    select = np.einsum("ci,hu,ta,rs,op->rtchopiuas", np.eye(HALF), eye, eye, eye, np.eye(HALF))
    select = select.reshape(2 * C * C, HALF, 8 * HALF)
    select = np.pad(select, ((0, 0), (0, 0), (0, LANES - 8 * HALF))).reshape(2 * C * C, -1)
    place = np.einsum(
        "or,pa,qb,lm->opqlmarb", np.eye(HALF), np.eye(PARTS), np.eye(QL), np.eye(LAYERS)
    )
    place = place.reshape(HALF * PARTS * QL * LAYERS, LAYERS * PARTS, HALF * QL)
    place = np.pad(place, ((0, 0), (0, 0), (0, LANES - HALF * QL)))
    place = place.reshape(HALF * PARTS * QL * LAYERS, -1)
    held = {
        "zt_fwd": zt_forward,
        "zt_inv": zt_inverse,
        "y_fwd": y_fwd,
        "y_inv": y_inv,
        "x_fwd": x_fwd,
        "x_inv": x_inv,
        "spread": spread,
        "select": select,
        "place": place,
    }
    return {name: table.astype(np.float32).astype(jnp.bfloat16) for name, table in held.items()}


def lane_index(shape):
    return lax.broadcasted_iota(jnp.int32, shape, len(shape) - 1)


def dot(left, right):
    return jnp.dot(left, right, preferred_element_type=jnp.float32)


def forward_step(step, block, zt_table, y_table, modes_ref):
    zt_fwd = zt_table[...]
    columns = []
    for pair in range(PAIRS):
        rows = []
        for half in range(2):
            z = dot(block(half, pair), zt_fwd).astype(jnp.bfloat16)
            rows += [z[:, :LANES], z[:, LANES:]]
        columns.append(jnp.concatenate(rows, 0))
    modes = dot(y_table[...], jnp.concatenate(columns, 1))
    lane = lane_index((MY * 8, LANES))
    for pair in range(PAIRS):
        channel = step * PAIRS + pair
        own = modes[:, pair * LANES : (pair + 1) * LANES]
        mask = (lane >= channel * QL) & (lane < channel * QL + QL)
        for qh in range(QH):
            shift = lax.rem((channel - qh) * QL + LANES, LANES)
            moved = pltpu.roll(own, shift, 1)
            kept = modes_ref[:, qh].reshape(MY * 8, LANES)
            modes_ref[:, qh] = jnp.where(mask, moved, kept).reshape(MY, 8, LANES)


def forward_kernel(field_ref, zt_ref, y_ref, out_ref, modes_ref):
    step = pl.program_id(0)

    @pl.when(step == 0)
    def _():
        modes_ref[...] = jnp.zeros_like(modes_ref)

    def block(half, pair):
        return field_ref[half, pair].reshape(PLANES * Y, ZT)

    forward_step(step, block, zt_ref, y_ref, modes_ref)

    @pl.when(step == STEPS - 1)
    def _():
        out_ref[...] = modes_ref[...].reshape(GROUPS * 8, LANES).astype(jnp.bfloat16)


IN_VMEM = pl.BlockSpec(memory_space=pltpu.VMEM)


def in_vmem(arrays):
    return [pltpu.with_memory_space_constraint(array, pltpu.VMEM) for array in arrays]


def in_hbm(array):
    return pltpu.with_memory_space_constraint(array, pltpu.HBM)


def whole(shape):
    return pl.BlockSpec(shape, lambda *_: (0,) * len(shape), pipeline_mode=pl.Buffered(1))


def field_spec():
    return pl.BlockSpec((2, PAIRS, PLANES, Y, ZT), lambda s: (0, s, 0, 0, 0))


MESSAGE = (GROUPS * 8, LANES)
MODES = pltpu.VMEM((MY, QH, 8, LANES), jnp.float32)


def forward_call(field, tables):
    return pl.pallas_call(
        forward_kernel,
        grid=(STEPS,),
        in_specs=[field_spec(), IN_VMEM, IN_VMEM],
        out_specs=whole(MESSAGE),
        out_shape=jax.ShapeDtypeStruct(MESSAGE, jnp.bfloat16),
        scratch_shapes=[MODES],
        compiler_params=pltpu.CompilerParams(vmem_limit_bytes=VMEM_BYTES),
        name="forward_zt_y",
    )(in_hbm(field), *in_vmem((tables["zt_fwd"], tables["y_fwd"])))


def gelu(x):
    s = jnp.minimum(x * x, ERF_LIMIT)
    p = jnp.float32(ERF_COEFFICIENTS[-1])
    for coefficient in ERF_COEFFICIENTS[-2::-1]:
        p = p * s + jnp.float32(coefficient)
    h = 0.5 * x
    return h + h * jnp.tanh(x * p)


def inverse_step(step, modes_ref, local_ref, y_table, zt_table, out_ref):
    lane = lane_index((MY * 8, LANES))
    columns = []
    for pair in range(PAIRS):
        channel = step * PAIRS + pair
        value = jnp.zeros((MY * 8, LANES), jnp.float32)
        for qh in range(QH):
            shift = lax.rem((qh - channel) * QL + LANES, LANES)
            moved = pltpu.roll(modes_ref[:, qh].reshape(MY * 8, LANES), shift, 1)
            value = jnp.where((lane >= qh * QL) & (lane < qh * QL + QL), moved, value)
        columns.append(value.astype(jnp.bfloat16))
    back = dot(y_table[...], jnp.concatenate(columns, 1)).astype(jnp.bfloat16)
    zt_inv = zt_table[...]
    span = PLANES * Y
    results = {}
    for pair in range(PAIRS):
        own = back[:, pair * LANES : (pair + 1) * LANES]
        for half in range(2):
            at = 2 * half * span
            rows = jnp.concatenate([own[at : at + span], own[at + span : at + 2 * span]], 1)
            total = dot(rows, zt_inv) + local_ref[half, pair].reshape(span, ZT)
            result = gelu(total).astype(jnp.bfloat16)
            out_ref[half, pair] = result.reshape(PLANES, Y, ZT)
            results[half, pair] = result
    return results


def load_modes(message_ref, modes_ref):
    modes_ref[...] = message_ref[...].astype(jnp.float32).reshape(MY, QH, 8, LANES)


def inverse_kernel(local_ref, message_ref, y_ref, zt_ref, out_ref, modes_ref):
    step = pl.program_id(0)

    @pl.when(step == 0)
    def _():
        load_modes(message_ref, modes_ref)

    inverse_step(step, modes_ref, local_ref, y_ref, zt_ref, out_ref)


FIELD = (2, HALF, PLANES, Y, ZT)


def inverse_call(message, local, tables):
    held = [message, tables["y_inv"], tables["zt_inv"]]
    return pl.pallas_call(
        inverse_kernel,
        grid=(STEPS,),
        in_specs=[field_spec()] + [IN_VMEM] * 3,
        out_specs=field_spec(),
        out_shape=pltpu.HBM(FIELD, jnp.bfloat16),
        scratch_shapes=[MODES],
        compiler_params=pltpu.CompilerParams(vmem_limit_bytes=VMEM_BYTES),
        name="inverse_zt_y",
    )(in_hbm(local), *in_vmem(held))


def turn_kernel(
    local_ref, message_ref, y_inv, zt_inv, zt_fwd, y_fwd, out_ref, send_ref, modes_ref, next_ref
):
    step = pl.program_id(0)

    @pl.when(step == 0)
    def _():
        load_modes(message_ref, modes_ref)
        next_ref[...] = jnp.zeros_like(next_ref)

    results = inverse_step(step, modes_ref, local_ref, y_inv, zt_inv, out_ref)

    def block(half, pair):
        return results[half, pair]

    forward_step(step, block, zt_fwd, y_fwd, next_ref)

    @pl.when(step == STEPS - 1)
    def _():
        send_ref[...] = next_ref[...].reshape(GROUPS * 8, LANES).astype(jnp.bfloat16)


def turn_call(message, local, tables):
    held = [message] + [tables[name] for name in ("y_inv", "zt_inv", "zt_fwd", "y_fwd")]
    return pl.pallas_call(
        turn_kernel,
        grid=(STEPS,),
        in_specs=[field_spec()] + [IN_VMEM] * len(held),
        out_specs=[field_spec(), whole(MESSAGE)],
        out_shape=[
            pltpu.HBM(FIELD, jnp.bfloat16),
            jax.ShapeDtypeStruct(MESSAGE, jnp.bfloat16),
        ],
        scratch_shapes=[MODES, MODES],
        compiler_params=pltpu.CompilerParams(vmem_limit_bytes=VMEM_BYTES),
        name="inverse_then_forward",
    )(in_hbm(local), *in_vmem(held))


def mix_kernel(
    place_ref, message_ref, x_table, spread_table, weights_ref, inv_ref, out_ref, sums_ref
):
    span = OWNERS * 8
    message = message_ref[...].astype(jnp.float32).reshape(OWNERS, PARTS * 8, LANES)
    pieces = [
        message[:, part * 8 : part * 8 + 8].reshape(span, LANES).astype(jnp.bfloat16)
        for part in range(PARTS)
    ]
    pieces = jnp.concatenate(pieces, 1)
    group_rows = 2 * ROWS
    for distance in range(KX_GROUPS):
        group = place_ref[0] ^ distance
        table = x_table[pl.ds(pl.multiple_of(group * group_rows, group_rows), group_rows), :]
        modes = dot(table, pieces).astype(jnp.bfloat16)
        rows = [modes[:, part * LANES : (part + 1) * LANES] for part in range(PARTS)]
        spread = dot(jnp.concatenate(rows, 0), spread_table[...])
        for part in range(PARTS):
            for out_half in range(2):
                totals = [None, None]
                for c10 in range(HALF):
                    at = ((c10 * PARTS + part) * 2 + out_half) * ROWS
                    weight = weights_ref[distance, at : at + ROWS, :].astype(jnp.float32)
                    for kind in range(2):
                        top = part * group_rows + kind * ROWS
                        term = spread[top : top + ROWS, c10 * LANES : (c10 + 1) * LANES] * weight
                        totals[kind] = term if c10 == 0 else totals[kind] + term
                for kind in range(2):
                    start = group * (4 * ROWS) + (kind * 2 + out_half) * ROWS
                    sums_ref[
                        pl.ds(pl.multiple_of(start, 8), ROWS), part * LANES : (part + 1) * LANES
                    ] = totals[kind]
    back = dot(inv_ref[...], sums_ref[...].astype(jnp.bfloat16))
    blocks = [
        back[:, part * LANES : (part + 1) * LANES].reshape(OWNERS, 8, LANES)
        for part in range(PARTS)
    ]
    out_ref[...] = jnp.concatenate(blocks, 1).reshape(GROUPS * 8, LANES).astype(jnp.bfloat16)


def mix_call(place, message, weights, tables):
    held = [message, tables["x_fwd"], tables["spread"], tables["x_inv"]]
    return pl.pallas_call(
        mix_kernel,
        grid=(1,),
        in_specs=[pl.BlockSpec(memory_space=pltpu.SMEM)] + [IN_VMEM] * 5,
        out_specs=whole(MESSAGE),
        out_shape=jax.ShapeDtypeStruct(MESSAGE, jnp.bfloat16),
        scratch_shapes=[pltpu.VMEM((KX_GROUPS * 4 * ROWS, PARTS * LANES), jnp.float32)],
        compiler_params=pltpu.CompilerParams(vmem_limit_bytes=VMEM_BYTES),
        name="mix_x",
    )(place, *in_vmem(held[:3] + [weights] + held[3:]))


WEIGHT_ROWS = HALF * PARTS * 2 * ROWS
WEIGHTS = (KX_GROUPS, WEIGHT_ROWS, LANES)


def arrange_kernel(own, near, far, across, select_ref, place_ref, first_ref, second_ref, rows_ref):
    rows = PARTS * QL * LAYERS
    for distance, weights in enumerate((own, near, far, across)):
        split = dot(weights[...].reshape(KX_PER * rows, 2 * C * C), select_ref[...])
        columns = []
        for kx in range(KX_PER):
            block = split[kx * rows : (kx + 1) * rows]
            stacked = [block[:, out * LANES : (out + 1) * LANES] for out in range(HALF)]
            columns.append(jnp.concatenate(stacked, 0).astype(jnp.bfloat16))
        moved = lax.dot_general(
            jnp.concatenate(columns, 1),
            place_ref[...],
            (((0,), (0,)), ((), ())),
            preferred_element_type=jnp.float32,
        )
        for layer, out_ref in enumerate((first_ref, second_ref)):
            for part in range(PARTS):
                lane = (layer * PARTS + part) * LANES
                for kx in range(KX_PER):
                    for c10 in range(HALF):
                        row = kx * LANES + c10 * 8
                        start = (c10 * PARTS + part) * 2 * ROWS + kx
                        rows_ref[layer, pl.ds(start, 8, stride=KX_PER), :] = moved[
                            row : row + 8, lane : lane + LANES
                        ]
            out_ref[distance] = rows_ref[layer].astype(jnp.bfloat16)


def arrange_weights(shards, tables):
    held = shards + [tables["select"], tables["place"]]
    return pl.pallas_call(
        arrange_kernel,
        grid=(1,),
        in_specs=[IN_VMEM] * len(held),
        out_specs=[IN_VMEM] * LAYERS,
        out_shape=[pltpu.VMEM(WEIGHTS, jnp.bfloat16)] * LAYERS,
        scratch_shapes=[pltpu.VMEM((LAYERS, WEIGHT_ROWS, LANES), jnp.float32)],
        compiler_params=pltpu.CompilerParams(vmem_limit_bytes=VMEM_BYTES),
        name="arrange_weights",
    )(*in_vmem(held))


def swap(value, distance):
    return lax.ppermute(value, "batch", [(i, i ^ distance) for i in range(KX_GROUPS)])


def gather_weights(weights):
    own = jnp.transpose(weights, (1, 2, 0, 3))
    far = swap(own, 2)
    return [own, swap(own, 1), far, swap(far, 1)]


def exchange(message):
    grouped = message.reshape(OWNERS, PARTS * 8, LANES)
    moved = lax.all_to_all(grouped, "space", split_axis=0, concat_axis=0, tiled=True)
    return moved.reshape(MESSAGE)


def local_kernel(offset_ref, weight_ref, field_ref, out_ref, mixing_ref):
    size = C * STRIP

    @pl.when((pl.program_id(0) == 0) & (pl.program_id(1) == 0))
    def _():
        row = lax.broadcasted_iota(jnp.int32, (size, C), 0) // STRIP
        pick_out = (row == lane_index((size, C))).astype(jnp.bfloat16)
        lane = lane_index((C, size)) // STRIP
        pick_in = (lax.broadcasted_iota(jnp.int32, (C, size), 0) == lane).astype(jnp.bfloat16)
        rows = dot(pick_out, weight_ref[...]).astype(jnp.bfloat16)
        full = dot(rows, pick_in)
        same = lax.rem(lax.broadcasted_iota(jnp.int32, (size, size), 0), STRIP) == lax.rem(
            lane_index((size, size)), STRIP
        )
        mixing_ref[...] = jnp.where(same, full, 0.0).astype(jnp.bfloat16)

    for first in range(0, LOCAL_ROWS, STRIP):
        mixed = dot(mixing_ref[...], field_ref[:, :, 0, first : first + STRIP].reshape(size, ZT))
        for half in range(2):
            for c10 in range(HALF):
                channel = half * HALF + c10
                rows = mixed[channel * STRIP : (channel + 1) * STRIP] + offset_ref[channel]
                out_ref[half, c10, 0, first : first + STRIP] = rows.astype(jnp.bfloat16)


def local_term(current, weight, offset):
    spec = pl.BlockSpec((2, HALF, 1, LOCAL_ROWS, ZT), lambda p, y: (0, 0, p, y, 0))
    return pl.pallas_call(
        local_kernel,
        grid=(PLANES, Y // LOCAL_ROWS),
        in_specs=[pl.BlockSpec(memory_space=pltpu.SMEM), whole((C, C)), spec],
        out_specs=spec,
        out_shape=pltpu.HBM(FIELD, jnp.bfloat16),
        scratch_shapes=[pltpu.VMEM((C * STRIP, C * STRIP), jnp.bfloat16)],
        compiler_params=pltpu.CompilerParams(vmem_limit_bytes=VMEM_BYTES),
        name="local_mixing",
    )(offset, weight.T, in_hbm(current))


def after(value, *others):
    return lax.optimization_barrier((value,) + others)[0]


def body(field, spectral_weight, local_weight, bias):
    tables = {name: jnp.asarray(table) for name, table in build_tables().items()}
    place = lax.axis_index("batch").astype(jnp.int32).reshape(1)
    field = field.reshape(FIELD)
    shards = gather_weights(spectral_weight)
    message = forward_call(field, tables)
    weights = arrange_weights(shards, dict(tables, place=after(tables["place"], message)))
    back = mix_call(place, exchange(message), weights[0], tables)
    local = local_term(field, after(local_weight[0], back), bias[0])
    current, message = turn_call(exchange(back), local, tables)
    local = local_term(current, local_weight[1], bias[1])
    back = mix_call(place, after(exchange(message), local), weights[1], tables)
    return inverse_call(exchange(back), local, tables).reshape(1, C, PLANES, Y, ZT)


def solution(mesh):
    placed = (P("batch", None, "space", None, None), P(None, "batch", "space", None), P(), P())
    return jax.shard_map(
        body,
        mesh=mesh,
        in_specs=placed,
        out_specs=P("batch", None, "space", None, None),
        check_vma=False,
    )
```

```python
import math

import jax
import jax.numpy as jnp
import numpy as np
from jax import lax
from jax.experimental import pallas as pl
from jax.experimental.pallas import tpu as pltpu
from jax.sharding import PartitionSpec as P

X = 128
Y = 128
VERTICAL_POINTS = 32
EPOCH_COUNT = 16
ZT = VERTICAL_POINTS * EPOCH_COUNT
C = 20
MX = 24
MY = 24
MZ = 12
MT = 8
LAYERS = 2

QL = 12
QH = MZ * MT // QL
GROUPS = MY * QH
PARTS = 3
HALF = C // 2
LANES = 128
PLANES = 2
OWNERS = X // PLANES
KX_GROUPS = 4
KX_PER = MX // KX_GROUPS
ROWS = 2 * 2 * KX_PER
PAIRS = 2
STEPS = HALF // PAIRS
STRIP = 16
LOCAL_ROWS = 64
VMEM_BYTES = 48 << 20

ERF_COEFFICIENTS = (
    7.97884216e-01,
    3.63342831e-02,
    -3.31296180e-05,
    -5.52402773e-05,
    3.96912621e-06,
    -1.33447465e-07,
    1.80564042e-09,
)
HALVED_COEFFICIENTS = tuple(2.0 * 4.0**i * c for i, c in enumerate(ERF_COEFFICIENTS))


def line_table(length, kept_count):
    half = kept_count // 2
    frequency = np.concatenate([np.arange(half), np.arange(length - half, length)])
    angles = 2.0 * math.pi / length * (np.arange(length)[:, None] * frequency[None, :] % length)
    cosine = np.cos(angles) / math.sqrt(length)
    sine = np.sin(angles) / math.sqrt(length)
    forward = np.stack([np.stack([cosine, -sine], 1), np.stack([sine, cosine], 1)], 1)
    inverse = np.stack([np.stack([cosine.T, sine.T], -1), np.stack([-sine.T, cosine.T], -1)], 1)
    return forward, inverse


def depth_table():
    half = MZ // 2
    vertical = np.concatenate([np.arange(half), np.arange(VERTICAL_POINTS - half, VERTICAL_POINTS)])
    clock = np.arange(MT)
    cells = np.arange(ZT)
    turns = (
        (cells // EPOCH_COUNT)[:, None, None] * vertical[None, :, None] * EPOCH_COUNT
        + (cells % EPOCH_COUNT)[:, None, None] * clock[None, None, :] * VERTICAL_POINTS
    ) % ZT
    angles = 2.0 * math.pi / ZT * turns.reshape(ZT, MZ * MT)
    cosine = np.cos(angles) / math.sqrt(ZT)
    sine = np.sin(angles) / math.sqrt(ZT)
    doubling = np.broadcast_to(np.where(clock == 0, 1.0, 2.0)[None, :], (MZ, MT)).reshape(-1)
    kept = MZ * MT
    forward = np.zeros((ZT, 2 * LANES))
    forward[:, :kept] = cosine
    forward[:, LANES : LANES + kept] = -sine
    inverse = np.zeros((2 * LANES, ZT))
    inverse[:kept] = cosine.T * doubling[:, None]
    inverse[LANES : LANES + kept] = -sine.T * doubling[:, None]
    return forward, 0.5 * inverse


def build_tables():
    zt_forward, zt_inverse = depth_table()
    y_forward, y_inverse = line_table(Y, MY)
    x_forward, x_inverse = line_table(X, MX)
    eye = np.eye(2)
    y_fwd = np.einsum("yrjm,ab,uv->maujbrvy", y_forward, eye, eye)
    y_fwd = y_fwd.reshape(MY * 8, 4 * PLANES * Y)
    y_inv = np.einsum("mryj,ab,uv->ajuymbvr", y_inverse, eye, eye)
    y_inv = y_inv.reshape(4 * PLANES * Y, MY * 8)
    x_split = x_forward.reshape(OWNERS, PLANES, 2, 2, KX_GROUPS, KX_PER)
    x_re, x_im = x_split[:, :, :, 0], x_split[:, :, :, 1]
    parts = np.stack([np.stack([x_re, -x_im]), np.stack([x_im, x_re])])
    x_fwd = np.einsum("stiurgm,ab->gsatmibur", parts, eye)
    x_fwd = x_fwd.reshape(KX_GROUPS * 2 * ROWS, OWNERS * 8)
    x_split = x_inverse.reshape(KX_GROUPS, KX_PER, 2, OWNERS, PLANES, 2)
    x_inv = np.einsum("gmsiuj,ab,c,t->iaujgsbctm", x_split, eye, np.ones(2), np.ones(2))
    x_inv = x_inv.reshape(OWNERS * 8, KX_GROUPS * 4 * ROWS)
    same = np.tile(np.eye(QL), (HALF, HALF))
    same = np.pad(same, (0, LANES - HALF * QL))
    select = np.einsum("ci,hu,ta,rs,op->rtchopiuas", np.eye(HALF), eye, eye, eye, np.eye(HALF))
    select = select.reshape(2 * C * C, HALF, 8 * HALF)
    select = np.pad(select, ((0, 0), (0, 0), (0, LANES - 8 * HALF))).reshape(2 * C * C, -1)
    place = np.einsum(
        "or,pa,qb,lm->opqlmarb", np.eye(HALF), np.eye(PARTS), np.eye(QL), np.eye(LAYERS)
    )
    place = place.reshape(HALF * PARTS * QL * LAYERS, LAYERS * PARTS, HALF * QL)
    place = np.pad(place, ((0, 0), (0, 0), (0, LANES - HALF * QL)))
    place = place.reshape(HALF * PARTS * QL * LAYERS, -1)
    held = {
        "zt_fwd": zt_forward,
        "zt_inv": zt_inverse,
        "y_fwd": y_fwd,
        "y_inv": y_inv,
        "x_fwd": x_fwd,
        "x_inv": x_inv,
        "same": same,
        "select": select,
        "place": place,
    }
    return {name: table.astype(np.float32).astype(jnp.bfloat16) for name, table in held.items()}


def lane_index(shape):
    return lax.broadcasted_iota(jnp.int32, shape, len(shape) - 1)


def dot(left, right):
    return jnp.dot(left, right, preferred_element_type=jnp.float32)


def forward_step(step, block, zt_table, y_table, modes_ref):
    zt_fwd = zt_table[...]
    columns = []
    for pair in range(PAIRS):
        rows = []
        for half in range(2):
            z = dot(block(half, pair), zt_fwd).astype(jnp.bfloat16)
            rows += [z[:, :LANES], z[:, LANES:]]
        columns.append(jnp.concatenate(rows, 0))
    modes = dot(y_table[...], jnp.concatenate(columns, 1))
    lane = lane_index((MY * 8, LANES))
    for pair in range(PAIRS):
        channel = step * PAIRS + pair
        own = modes[:, pair * LANES : (pair + 1) * LANES]
        mask = (lane >= channel * QL) & (lane < channel * QL + QL)
        for qh in range(QH):
            shift = lax.rem((channel - qh) * QL + LANES, LANES)
            moved = pltpu.roll(own, shift, 1)
            kept = modes_ref[:, qh].reshape(MY * 8, LANES)
            modes_ref[:, qh] = jnp.where(mask, moved, kept).reshape(MY, 8, LANES)


def forward_kernel(field_ref, zt_ref, y_ref, out_ref, modes_ref):
    step = pl.program_id(0)

    @pl.when(step == 0)
    def _():
        modes_ref[...] = jnp.zeros_like(modes_ref)

    def block(half, pair):
        return field_ref[half, pair].reshape(PLANES * Y, ZT)

    forward_step(step, block, zt_ref, y_ref, modes_ref)

    @pl.when(step == STEPS - 1)
    def _():
        out_ref[...] = modes_ref[...].reshape(GROUPS * 8, LANES).astype(jnp.bfloat16)


IN_VMEM = pl.BlockSpec(memory_space=pltpu.VMEM)
IN_HBM = pl.BlockSpec(memory_space=pltpu.HBM)


def in_vmem(arrays):
    return [pltpu.with_memory_space_constraint(array, pltpu.VMEM) for array in arrays]


def in_hbm(array):
    return pltpu.with_memory_space_constraint(array, pltpu.HBM)


def whole(shape):
    return pl.BlockSpec(shape, lambda *_: (0,) * len(shape), pipeline_mode=pl.Buffered(1))


def field_spec():
    return pl.BlockSpec((2, PAIRS, PLANES, Y, ZT), lambda s: (0, s, 0, 0, 0))


MESSAGE = (GROUPS * 8, LANES)
MODES = pltpu.VMEM((MY, QH, 8, LANES), jnp.float32)


def forward_call(field, tables):
    return pl.pallas_call(
        forward_kernel,
        grid=(STEPS,),
        in_specs=[field_spec(), IN_VMEM, IN_VMEM],
        out_specs=whole(MESSAGE),
        out_shape=pltpu.HBM(MESSAGE, jnp.bfloat16),
        scratch_shapes=[MODES],
        compiler_params=pltpu.CompilerParams(vmem_limit_bytes=VMEM_BYTES),
        name="forward_zt_y",
    )(in_hbm(field), *in_vmem((tables["zt_fwd"], tables["y_fwd"])))


def gelu(h):
    s = h * h
    p = jnp.float32(HALVED_COEFFICIENTS[-1])
    for coefficient in HALVED_COEFFICIENTS[-2::-1]:
        p = p * s + jnp.float32(coefficient)
    return h + h * jnp.tanh(h * p)


def inverse_step(step, modes_ref, local_ref, y_table, zt_table, out_ref):
    lane = lane_index((MY * 8, LANES))
    columns = []
    for pair in range(PAIRS):
        channel = step * PAIRS + pair
        value = jnp.zeros((MY * 8, LANES), jnp.float32)
        for qh in range(QH):
            shift = lax.rem((qh - channel) * QL + LANES, LANES)
            moved = pltpu.roll(modes_ref[:, qh].reshape(MY * 8, LANES), shift, 1)
            value = jnp.where((lane >= qh * QL) & (lane < qh * QL + QL), moved, value)
        columns.append(value.astype(jnp.bfloat16))
    back = dot(y_table[...], jnp.concatenate(columns, 1)).astype(jnp.bfloat16)
    zt_inv = zt_table[...]
    span = PLANES * Y
    results = {}
    for pair in range(PAIRS):
        own = back[:, pair * LANES : (pair + 1) * LANES]
        for half in range(2):
            at = 2 * half * span
            rows = jnp.concatenate([own[at : at + span], own[at + span : at + 2 * span]], 1)
            total = dot(rows, zt_inv) + local_ref[half, pair].reshape(span, ZT)
            result = gelu(total).astype(jnp.bfloat16)
            out_ref[half, pair] = result.reshape(PLANES, Y, ZT)
            results[half, pair] = result
    return results


def load_modes(message_ref, modes_ref):
    modes_ref[...] = message_ref[...].astype(jnp.float32).reshape(MY, QH, 8, LANES)


def inverse_kernel(local_ref, message_ref, y_ref, zt_ref, out_ref, modes_ref):
    step = pl.program_id(0)

    @pl.when(step == 0)
    def _():
        load_modes(message_ref, modes_ref)

    inverse_step(step, modes_ref, local_ref, y_ref, zt_ref, out_ref)


FIELD = (2, HALF, PLANES, Y, ZT)


def inverse_call(message, local, tables):
    held = [message, tables["y_inv"], tables["zt_inv"]]
    return pl.pallas_call(
        inverse_kernel,
        grid=(STEPS,),
        in_specs=[field_spec()] + [IN_VMEM] * 3,
        out_specs=field_spec(),
        out_shape=pltpu.HBM(FIELD, jnp.bfloat16),
        scratch_shapes=[MODES],
        compiler_params=pltpu.CompilerParams(vmem_limit_bytes=VMEM_BYTES),
        name="inverse_zt_y",
    )(in_hbm(local), *in_vmem(held))


def turn_kernel(
    local_ref, message_ref, y_inv, zt_inv, zt_fwd, y_fwd, out_ref, send_ref, modes_ref, next_ref
):
    step = pl.program_id(0)

    @pl.when(step == 0)
    def _():
        load_modes(message_ref, modes_ref)
        next_ref[...] = jnp.zeros_like(next_ref)

    results = inverse_step(step, modes_ref, local_ref, y_inv, zt_inv, out_ref)

    def block(half, pair):
        return results[half, pair]

    forward_step(step, block, zt_fwd, y_fwd, next_ref)

    @pl.when(step == STEPS - 1)
    def _():
        send_ref[...] = next_ref[...].reshape(GROUPS * 8, LANES).astype(jnp.bfloat16)


def turn_call(message, local, tables):
    held = [message] + [tables[name] for name in ("y_inv", "zt_inv", "zt_fwd", "y_fwd")]
    return pl.pallas_call(
        turn_kernel,
        grid=(STEPS,),
        in_specs=[field_spec()] + [IN_VMEM] * len(held),
        out_specs=[field_spec(), whole(MESSAGE)],
        out_shape=[
            pltpu.HBM(FIELD, jnp.bfloat16),
            pltpu.HBM(MESSAGE, jnp.bfloat16),
        ],
        scratch_shapes=[MODES, MODES],
        compiler_params=pltpu.CompilerParams(vmem_limit_bytes=VMEM_BYTES),
        name="inverse_then_forward",
    )(in_hbm(local), *in_vmem(held))


def mix_kernel(
    place_ref, message_ref, x_hbm, same_hbm, inv_hbm, weights_hbm, out_ref, sums_ref, x_table,
    same_ref, inv_ref, weights_ref, arrived
):
    pairs = [(x_hbm, x_table), (same_hbm, same_ref)]
    pairs += [(weights_hbm.at[i], weights_ref.at[i]) for i in range(KX_GROUPS)]
    pairs.append((inv_hbm, inv_ref))
    copies = [
        pltpu.make_async_copy(source, target, arrived.at[i])
        for i, (source, target) in enumerate(pairs)
    ]
    for copy in copies:
        copy.start()
    span = OWNERS * 8
    message = message_ref[...].astype(jnp.float32).reshape(OWNERS, PARTS * 8, LANES)
    pieces = [
        message[:, part * 8 : part * 8 + 8].reshape(span, LANES).astype(jnp.bfloat16)
        for part in range(PARTS)
    ]
    pieces = jnp.concatenate(pieces, 1)
    copies[0].wait()
    copies[1].wait()
    same = same_ref[...].astype(jnp.float32)
    row = lax.broadcasted_iota(jnp.int32, same.shape, 0)
    spread_table = [
        jnp.where((row >= c10 * QL) & (row < c10 * QL + QL), same, 0.0) for c10 in range(HALF)
    ]
    spread_table = jnp.concatenate(spread_table, 1).astype(jnp.bfloat16)
    group_rows = 2 * ROWS
    for distance in range(KX_GROUPS):
        group = place_ref[0] ^ distance
        table = x_table[pl.ds(pl.multiple_of(group * group_rows, group_rows), group_rows), :]
        modes = dot(table, pieces).astype(jnp.bfloat16)
        rows = [modes[:, part * LANES : (part + 1) * LANES] for part in range(PARTS)]
        spread = dot(jnp.concatenate(rows, 0), spread_table)
        copies[2 + distance].wait()
        for part in range(PARTS):
            for out_half in range(2):
                totals = [None, None]
                for c10 in range(HALF):
                    at = ((c10 * PARTS + part) * 2 + out_half) * ROWS
                    weight = weights_ref[distance, at : at + ROWS, :].astype(jnp.float32)
                    for kind in range(2):
                        top = part * group_rows + kind * ROWS
                        term = spread[top : top + ROWS, c10 * LANES : (c10 + 1) * LANES] * weight
                        totals[kind] = term if c10 == 0 else totals[kind] + term
                for kind in range(2):
                    start = group * (4 * ROWS) + (kind * 2 + out_half) * ROWS
                    sums_ref[
                        pl.ds(pl.multiple_of(start, 8), ROWS), part * LANES : (part + 1) * LANES
                    ] = totals[kind]
    copies[6].wait()
    back = dot(inv_ref[...], sums_ref[...].astype(jnp.bfloat16))
    blocks = [
        back[:, part * LANES : (part + 1) * LANES].reshape(OWNERS, 8, LANES)
        for part in range(PARTS)
    ]
    out_ref[...] = jnp.concatenate(blocks, 1).reshape(GROUPS * 8, LANES).astype(jnp.bfloat16)


def mix_call(place, message, weights, tables):
    held = [tables["x_fwd"], tables["same"], tables["x_inv"]]
    return pl.pallas_call(
        mix_kernel,
        grid=(1,),
        in_specs=[pl.BlockSpec(memory_space=pltpu.SMEM), IN_VMEM] + [IN_HBM] * 4,
        out_specs=whole(MESSAGE),
        out_shape=pltpu.HBM(MESSAGE, jnp.bfloat16),
        scratch_shapes=[pltpu.VMEM((KX_GROUPS * 4 * ROWS, PARTS * LANES), jnp.float32)]
        + [pltpu.VMEM(table.shape, table.dtype) for table in held]
        + [pltpu.VMEM(WEIGHTS, jnp.bfloat16), pltpu.SemaphoreType.DMA((7,))],
        compiler_params=pltpu.CompilerParams(vmem_limit_bytes=VMEM_BYTES),
        name="mix_x",
    )(place, *in_vmem([message]), *map(in_hbm, held + [weights]))


WEIGHT_ROWS = HALF * PARTS * 2 * ROWS
WEIGHTS = (KX_GROUPS, WEIGHT_ROWS, LANES)


def arrange_kernel(
    own, near, far, across, select_ref, place_ref, first_ref, second_ref, shards_ref, rows_ref, done_ref, arrived, left
):
    rows = PARTS * QL * LAYERS
    arriving = [
        pltpu.make_async_copy(shard, shards_ref.at[i], arrived.at[i])
        for i, shard in enumerate((own, near, far, across))
    ]
    for copy in arriving:
        copy.start()
    leaving = []
    for distance in range(KX_GROUPS):
        arriving[distance].wait()
        split = dot(shards_ref[distance].reshape(KX_PER * rows, 2 * C * C), select_ref[...])
        columns = []
        for kx in range(KX_PER):
            block = split[kx * rows : (kx + 1) * rows]
            stacked = [block[:, out * LANES : (out + 1) * LANES] for out in range(HALF)]
            columns.append(jnp.concatenate(stacked, 0).astype(jnp.bfloat16))
        moved = lax.dot_general(
            jnp.concatenate(columns, 1),
            place_ref[...],
            (((0,), (0,)), ((), ())),
            preferred_element_type=jnp.float32,
        )
        for layer, out_ref in enumerate((first_ref, second_ref)):
            for part in range(PARTS):
                lane = (layer * PARTS + part) * LANES
                for kx in range(KX_PER):
                    for c10 in range(HALF):
                        row = kx * LANES + c10 * 8
                        start = (c10 * PARTS + part) * 2 * ROWS + kx
                        rows_ref[layer, pl.ds(start, 8, stride=KX_PER), :] = moved[
                            row : row + 8, lane : lane + LANES
                        ]
            done_ref[layer, distance] = rows_ref[layer].astype(jnp.bfloat16)
            copy = pltpu.make_async_copy(
                done_ref.at[layer, distance], out_ref.at[distance], left.at[layer, distance]
            )
            copy.start()
            leaving.append(copy)
    for copy in leaving:
        copy.wait()


def arrange_weights(shards, tables):
    held = [tables["select"], tables["place"]]
    return pl.pallas_call(
        arrange_kernel,
        grid=(1,),
        in_specs=[IN_HBM] * KX_GROUPS + [IN_VMEM] * 2,
        out_specs=[IN_HBM] * LAYERS,
        out_shape=[pltpu.HBM(WEIGHTS, jnp.bfloat16)] * LAYERS,
        scratch_shapes=[
            pltpu.VMEM((KX_GROUPS,) + shards[0].shape, shards[0].dtype),
            pltpu.VMEM((LAYERS, WEIGHT_ROWS, LANES), jnp.float32),
            pltpu.VMEM((LAYERS,) + WEIGHTS, jnp.bfloat16),
            pltpu.SemaphoreType.DMA((KX_GROUPS,)),
            pltpu.SemaphoreType.DMA((LAYERS, KX_GROUPS)),
        ],
        compiler_params=pltpu.CompilerParams(vmem_limit_bytes=VMEM_BYTES),
        name="arrange_weights",
    )(*map(in_hbm, shards), *in_vmem(held))


def swap(value, distance):
    return lax.ppermute(value, "batch", [(i, i ^ distance) for i in range(KX_GROUPS)])


def gather_weights(weights):
    own = jnp.transpose(weights, (1, 2, 0, 3))
    far = swap(own, 2)
    return [own, swap(own, 1), far, swap(far, 1)]


def exchange(message):
    grouped = message.reshape(OWNERS, PARTS * 8, LANES)
    moved = lax.all_to_all(grouped, "space", split_axis=0, concat_axis=0, tiled=True)
    return moved.reshape(MESSAGE)


def local_kernel(offset_ref, weight_ref, field_ref, out_ref, mixing_ref):
    size = C * STRIP

    @pl.when((pl.program_id(0) == 0) & (pl.program_id(1) == 0))
    def _():
        row = lax.broadcasted_iota(jnp.int32, (size, C), 0) // STRIP
        pick_out = (row == lane_index((size, C))).astype(jnp.bfloat16)
        lane = lane_index((C, size)) // STRIP
        pick_in = (lax.broadcasted_iota(jnp.int32, (C, size), 0) == lane).astype(jnp.bfloat16)
        rows = dot(pick_out, weight_ref[...]).astype(jnp.bfloat16)
        full = dot(rows, pick_in)
        same = lax.rem(lax.broadcasted_iota(jnp.int32, (size, size), 0), STRIP) == lax.rem(
            lane_index((size, size)), STRIP
        )
        mixing_ref[...] = jnp.where(same, full, 0.0).astype(jnp.bfloat16)

    for first in range(0, LOCAL_ROWS, STRIP):
        mixed = dot(mixing_ref[...], field_ref[:, :, 0, first : first + STRIP].reshape(size, ZT))
        for half in range(2):
            for c10 in range(HALF):
                channel = half * HALF + c10
                rows = mixed[channel * STRIP : (channel + 1) * STRIP] + 0.5 * offset_ref[channel]
                out_ref[half, c10, 0, first : first + STRIP] = rows.astype(jnp.bfloat16)


def local_term(current, weight, offset):
    spec = pl.BlockSpec((2, HALF, 1, LOCAL_ROWS, ZT), lambda p, y: (0, 0, p, y, 0))
    return pl.pallas_call(
        local_kernel,
        grid=(PLANES, Y // LOCAL_ROWS),
        in_specs=[pl.BlockSpec(memory_space=pltpu.SMEM), whole((C, C)), spec],
        out_specs=spec,
        out_shape=pltpu.HBM(FIELD, jnp.bfloat16),
        scratch_shapes=[pltpu.VMEM((C * STRIP, C * STRIP), jnp.bfloat16)],
        compiler_params=pltpu.CompilerParams(vmem_limit_bytes=VMEM_BYTES),
        name="local_mixing",
    )(offset, (0.5 * weight).T, in_hbm(current))


def after(value, *others):
    return lax.optimization_barrier((value,) + others)[0]


def body(field, spectral_weight, local_weight, bias):
    tables = {name: jnp.asarray(table) for name, table in build_tables().items()}
    place = lax.axis_index("batch").astype(jnp.int32).reshape(1)
    field = field.reshape(FIELD)
    own, near, far, across = gather_weights(spectral_weight)
    message = forward_call(field, tables)
    weights = arrange_weights([after(own, message), near, far, across], tables)
    back = mix_call(place, exchange(message), weights[0], tables)
    local = local_term(field, after(local_weight[0], back), bias[0])
    current, message = turn_call(exchange(back), local, tables)
    local = local_term(current, local_weight[1], bias[1])
    back = mix_call(place, after(exchange(message), local), weights[1], tables)
    return inverse_call(exchange(back), local, tables).reshape(1, C, PLANES, Y, ZT)


def solution(mesh):
    placed = (P("batch", None, "space", None, None), P(None, "batch", "space", None), P(), P())
    return jax.shard_map(
        body,
        mesh=mesh,
        in_specs=placed,
        out_specs=P("batch", None, "space", None, None),
        check_vma=False,
    )
```

```python
import math

import jax
import jax.numpy as jnp
import numpy as np
from jax import lax
from jax.experimental import pallas as pl
from jax.experimental.pallas import tpu as pltpu
from jax.sharding import PartitionSpec as P

X = 128
Y = 128
VERTICAL_POINTS = 32
EPOCH_COUNT = 16
ZT = VERTICAL_POINTS * EPOCH_COUNT
C = 20
MX = 24
MY = 24
MZ = 12
MT = 8
LAYERS = 2

QL = 12
QH = MZ * MT // QL
GROUPS = MY * QH
PARTS = 3
HALF = C // 2
LANES = 128
PLANES = 2
OWNERS = X // PLANES
KX_GROUPS = 4
KX_PER = MX // KX_GROUPS
ROWS = 2 * 2 * KX_PER
PAIRS = 2
STEPS = HALF // PAIRS
STRIP = 16
LOCAL_ROWS = 64
VMEM_BYTES = 48 << 20

ERF_COEFFICIENTS = (
    7.97884216e-01,
    3.63342831e-02,
    -3.31296180e-05,
    -5.52402773e-05,
    3.96912621e-06,
    -1.33447465e-07,
    1.80564042e-09,
)
HALVED_COEFFICIENTS = tuple(2.0 * 4.0**i * c for i, c in enumerate(ERF_COEFFICIENTS))


def line_table(length, kept_count):
    half = kept_count // 2
    frequency = np.concatenate([np.arange(half), np.arange(length - half, length)])
    angles = 2.0 * math.pi / length * (np.arange(length)[:, None] * frequency[None, :] % length)
    cosine = np.cos(angles) / math.sqrt(length)
    sine = np.sin(angles) / math.sqrt(length)
    forward = np.stack([np.stack([cosine, -sine], 1), np.stack([sine, cosine], 1)], 1)
    inverse = np.stack([np.stack([cosine.T, sine.T], -1), np.stack([-sine.T, cosine.T], -1)], 1)
    return forward, inverse


def depth_table():
    half = MZ // 2
    vertical = np.concatenate([np.arange(half), np.arange(VERTICAL_POINTS - half, VERTICAL_POINTS)])
    clock = np.arange(MT)
    cells = np.arange(ZT)
    turns = (
        (cells // EPOCH_COUNT)[:, None, None] * vertical[None, :, None] * EPOCH_COUNT
        + (cells % EPOCH_COUNT)[:, None, None] * clock[None, None, :] * VERTICAL_POINTS
    ) % ZT
    angles = 2.0 * math.pi / ZT * turns.reshape(ZT, MZ * MT)
    cosine = np.cos(angles) / math.sqrt(ZT)
    sine = np.sin(angles) / math.sqrt(ZT)
    doubling = np.broadcast_to(np.where(clock == 0, 1.0, 2.0)[None, :], (MZ, MT)).reshape(-1)
    kept = MZ * MT
    forward = np.zeros((ZT, 2 * LANES))
    forward[:, :kept] = cosine
    forward[:, LANES : LANES + kept] = -sine
    inverse = np.zeros((2 * LANES, ZT))
    inverse[:kept] = cosine.T * doubling[:, None]
    inverse[LANES : LANES + kept] = -sine.T * doubling[:, None]
    return forward, 0.5 * inverse


def build_tables():
    zt_forward, zt_inverse = depth_table()
    y_forward, y_inverse = line_table(Y, MY)
    x_forward, x_inverse = line_table(X, MX)
    eye = np.eye(2)
    y_fwd = np.einsum("yrjm,ab,uv->maujbrvy", y_forward, eye, eye)
    y_fwd = y_fwd.reshape(MY * 8, 4 * PLANES * Y)
    y_inv = np.einsum("mryj,ab,uv->ajuymbvr", y_inverse, eye, eye)
    y_inv = y_inv.reshape(4 * PLANES * Y, MY * 8)
    x_split = x_forward.reshape(OWNERS, PLANES, 2, 2, KX_GROUPS, KX_PER)
    x_re, x_im = x_split[:, :, :, 0], x_split[:, :, :, 1]
    parts = np.stack([np.stack([x_re, -x_im]), np.stack([x_im, x_re])])
    x_fwd = np.einsum("stiurgm,ab->gsatmibur", parts, eye)
    x_fwd = x_fwd.reshape(KX_GROUPS * 2 * ROWS, OWNERS * 8)
    x_split = x_inverse.reshape(KX_GROUPS, KX_PER, 2, OWNERS, PLANES, 2)
    x_inv = np.einsum("gmsiuj,ab,c,t->iaujgsbctm", x_split, eye, np.ones(2), np.ones(2))
    x_inv = x_inv.reshape(OWNERS * 8, KX_GROUPS * 4 * ROWS)
    same = np.tile(np.eye(QL), (HALF, HALF))
    same = np.pad(same, (0, LANES - HALF * QL))
    select = np.einsum("ci,hu,ta,rs,op->rtchopiuas", np.eye(HALF), eye, eye, eye, np.eye(HALF))
    select = select.reshape(2 * C * C, HALF, 8 * HALF)
    select = np.pad(select, ((0, 0), (0, 0), (0, LANES - 8 * HALF))).reshape(2 * C * C, -1)
    place = np.einsum(
        "or,pa,qb,lm->opqlmarb", np.eye(HALF), np.eye(PARTS), np.eye(QL), np.eye(LAYERS)
    )
    place = place.reshape(HALF * PARTS * QL * LAYERS, LAYERS * PARTS, HALF * QL)
    place = np.pad(place, ((0, 0), (0, 0), (0, LANES - HALF * QL)))
    place = place.reshape(HALF * PARTS * QL * LAYERS, -1)
    held = {
        "zt_fwd": zt_forward,
        "zt_inv": zt_inverse,
        "y_fwd": y_fwd,
        "y_inv": y_inv,
        "x_fwd": x_fwd,
        "x_inv": x_inv,
        "same": same,
        "select": select,
        "place": place,
    }
    return {name: table.astype(np.float32).astype(jnp.bfloat16) for name, table in held.items()}


def lane_index(shape):
    return lax.broadcasted_iota(jnp.int32, shape, len(shape) - 1)


def dot(left, right):
    return jnp.dot(left, right, preferred_element_type=jnp.float32)


def forward_step(step, block, zt_table, y_table, modes_ref):
    zt_fwd = zt_table[...]
    columns = []
    for pair in range(PAIRS):
        rows = []
        for half in range(2):
            z = dot(block(half, pair), zt_fwd).astype(jnp.bfloat16)
            rows += [z[:, :LANES], z[:, LANES:]]
        columns.append(jnp.concatenate(rows, 0))
    modes = dot(y_table[...], jnp.concatenate(columns, 1))
    for pair in range(PAIRS):
        modes_ref[step * PAIRS + pair] = modes[:, pair * LANES : (pair + 1) * LANES]


def group_masks():
    lane = lane_index((MY * 8, LANES))
    return [(lane >= g * QL) & (lane < g * QL + QL) for g in range(HALF)]


OFFSETS = range(1 - QH, HALF)


def pack_modes(modes_ref, turned_ref):
    masks = group_masks()
    for place, offset in enumerate(OFFSETS):
        value = jnp.zeros((MY * 8, LANES), jnp.float32)
        for qh in range(QH):
            if 0 <= qh + offset < HALF:
                value = jnp.where(masks[qh], modes_ref[qh + offset], value)
        turned_ref[place] = pltpu.roll(value, offset * QL % LANES, 1)
    strips = []
    for qh in range(QH):
        value = jnp.zeros((MY * 8, LANES), jnp.float32)
        for channel in range(HALF):
            value = jnp.where(masks[channel], turned_ref[channel - qh + QH - 1], value)
        strips.append(value.reshape(MY, 1, 8, LANES))
    return jnp.concatenate(strips, 1).reshape(GROUPS * 8, LANES).astype(jnp.bfloat16)


def unpack_modes(message_ref, modes_ref, turned_ref):
    masks = group_masks()
    message = message_ref[...].astype(jnp.float32).reshape(MY, QH, 8, LANES)
    strips = [message[:, qh].reshape(MY * 8, LANES) for qh in range(QH)]
    for place, offset in enumerate(OFFSETS):
        value = jnp.zeros((MY * 8, LANES), jnp.float32)
        for qh in range(QH):
            if 0 <= qh + offset < HALF:
                value = jnp.where(masks[qh + offset], strips[qh], value)
        turned_ref[place] = pltpu.roll(value, -offset * QL % LANES, 1)
    for channel in range(HALF):
        value = jnp.zeros((MY * 8, LANES), jnp.float32)
        for qh in range(QH):
            value = jnp.where(masks[qh], turned_ref[channel - qh + QH - 1], value)
        modes_ref[channel] = value.astype(jnp.bfloat16)


def forward_kernel(field_ref, zt_ref, y_ref, out_ref, modes_ref, turned_ref):
    step = pl.program_id(0)

    def block(half, pair):
        return field_ref[half, pair].reshape(PLANES * Y, ZT)

    forward_step(step, block, zt_ref, y_ref, modes_ref)

    @pl.when(step == STEPS - 1)
    def _():
        out_ref[...] = pack_modes(modes_ref, turned_ref)


IN_VMEM = pl.BlockSpec(memory_space=pltpu.VMEM)
IN_HBM = pl.BlockSpec(memory_space=pltpu.HBM)


def in_vmem(arrays):
    return [pltpu.with_memory_space_constraint(array, pltpu.VMEM) for array in arrays]


def in_hbm(array):
    return pltpu.with_memory_space_constraint(array, pltpu.HBM)


def whole(shape):
    return pl.BlockSpec(shape, lambda *_: (0,) * len(shape), pipeline_mode=pl.Buffered(1))


def field_spec():
    return pl.BlockSpec((2, PAIRS, PLANES, Y, ZT), lambda s: (0, s, 0, 0, 0))


MESSAGE = (GROUPS * 8, LANES)
SENT_MODES = pltpu.VMEM((HALF, MY * 8, LANES), jnp.float32)
GOT_MODES = pltpu.VMEM((HALF, MY * 8, LANES), jnp.bfloat16)
TURNED = pltpu.VMEM((len(OFFSETS), MY * 8, LANES), jnp.float32)


def forward_call(field, tables):
    return pl.pallas_call(
        forward_kernel,
        grid=(STEPS,),
        in_specs=[field_spec()] + [whole(tables[name].shape) for name in ("zt_fwd", "y_fwd")],
        out_specs=whole(MESSAGE),
        out_shape=pltpu.HBM(MESSAGE, jnp.bfloat16),
        scratch_shapes=[SENT_MODES, TURNED],
        compiler_params=pltpu.CompilerParams(vmem_limit_bytes=VMEM_BYTES),
        name="forward_zt_y",
    )(in_hbm(field), in_hbm(tables["zt_fwd"]), in_hbm(tables["y_fwd"]))


def gelu(h):
    s = h * h
    p = jnp.float32(HALVED_COEFFICIENTS[-1])
    for coefficient in HALVED_COEFFICIENTS[-2::-1]:
        p = p * s + jnp.float32(coefficient)
    return h + h * jnp.tanh(h * p)


def inverse_step(step, modes_ref, local_ref, y_table, zt_table, out_ref):
    columns = [modes_ref[step * PAIRS + pair] for pair in range(PAIRS)]
    back = dot(y_table[...], jnp.concatenate(columns, 1)).astype(jnp.bfloat16)
    zt_inv = zt_table[...]
    span = PLANES * Y
    results = {}
    for pair in range(PAIRS):
        own = back[:, pair * LANES : (pair + 1) * LANES]
        for half in range(2):
            at = 2 * half * span
            rows = jnp.concatenate([own[at : at + span], own[at + span : at + 2 * span]], 1)
            total = dot(rows, zt_inv) + local_ref[half, pair].reshape(span, ZT)
            result = gelu(total).astype(jnp.bfloat16)
            out_ref[half, pair] = result.reshape(PLANES, Y, ZT)
            results[half, pair] = result
    return results


def inverse_kernel(local_ref, message_ref, y_ref, zt_ref, out_ref, modes_ref, turned_ref):
    step = pl.program_id(0)

    @pl.when(step == 0)
    def _():
        unpack_modes(message_ref, modes_ref, turned_ref)

    inverse_step(step, modes_ref, local_ref, y_ref, zt_ref, out_ref)


FIELD = (2, HALF, PLANES, Y, ZT)


def inverse_call(message, local, tables):
    held = [message, tables["y_inv"], tables["zt_inv"]]
    return pl.pallas_call(
        inverse_kernel,
        grid=(STEPS,),
        in_specs=[field_spec()] + [IN_VMEM] * 3,
        out_specs=field_spec(),
        out_shape=pltpu.HBM(FIELD, jnp.bfloat16),
        scratch_shapes=[GOT_MODES, TURNED],
        compiler_params=pltpu.CompilerParams(vmem_limit_bytes=VMEM_BYTES),
        name="inverse_zt_y",
    )(in_hbm(local), *in_vmem(held))


def turn_kernel(
    local_ref, message_ref, y_inv, zt_inv, zt_fwd, y_fwd, out_ref, send_ref, modes_ref, next_ref, turned_ref
):
    step = pl.program_id(0)

    @pl.when(step == 0)
    def _():
        unpack_modes(message_ref, modes_ref, turned_ref)

    results = inverse_step(step, modes_ref, local_ref, y_inv, zt_inv, out_ref)

    def block(half, pair):
        return results[half, pair]

    forward_step(step, block, zt_fwd, y_fwd, next_ref)

    @pl.when(step == STEPS - 1)
    def _():
        send_ref[...] = pack_modes(next_ref, turned_ref)


def turn_call(message, local, tables):
    held = [message] + [tables[name] for name in ("y_inv", "zt_inv", "zt_fwd", "y_fwd")]
    return pl.pallas_call(
        turn_kernel,
        grid=(STEPS,),
        in_specs=[field_spec()] + [IN_VMEM] * len(held),
        out_specs=[field_spec(), whole(MESSAGE)],
        out_shape=[
            pltpu.HBM(FIELD, jnp.bfloat16),
            pltpu.HBM(MESSAGE, jnp.bfloat16),
        ],
        scratch_shapes=[GOT_MODES, SENT_MODES, TURNED],
        compiler_params=pltpu.CompilerParams(vmem_limit_bytes=VMEM_BYTES),
        name="inverse_then_forward",
    )(in_hbm(local), *in_vmem(held))


def mix_kernel(
    place_ref, message_ref, x_hbm, same_hbm, inv_hbm, weights_hbm, out_ref, sums_ref, x_table,
    same_ref, inv_ref, weights_ref, arrived
):
    pairs = [(x_hbm, x_table), (same_hbm, same_ref)]
    pairs += [(weights_hbm.at[i], weights_ref.at[i]) for i in range(KX_GROUPS)]
    pairs.append((inv_hbm, inv_ref))
    copies = [
        pltpu.make_async_copy(source, target, arrived.at[i])
        for i, (source, target) in enumerate(pairs)
    ]
    for copy in copies:
        copy.start()
    span = OWNERS * 8
    message = message_ref[...].astype(jnp.float32).reshape(OWNERS, PARTS * 8, LANES)
    pieces = [
        message[:, part * 8 : part * 8 + 8].reshape(span, LANES).astype(jnp.bfloat16)
        for part in range(PARTS)
    ]
    pieces = jnp.concatenate(pieces, 1)
    copies[0].wait()
    copies[1].wait()
    same = same_ref[...].astype(jnp.float32)
    row = lax.broadcasted_iota(jnp.int32, same.shape, 0)
    spread_table = [
        jnp.where((row >= c10 * QL) & (row < c10 * QL + QL), same, 0.0) for c10 in range(HALF)
    ]
    spread_table = jnp.concatenate(spread_table, 1).astype(jnp.bfloat16)
    group_rows = 2 * ROWS
    for distance in range(KX_GROUPS):
        group = place_ref[0] ^ distance
        table = x_table[pl.ds(pl.multiple_of(group * group_rows, group_rows), group_rows), :]
        modes = dot(table, pieces).astype(jnp.bfloat16)
        rows = [modes[:, part * LANES : (part + 1) * LANES] for part in range(PARTS)]
        spread = dot(jnp.concatenate(rows, 0), spread_table)
        copies[2 + distance].wait()
        for part in range(PARTS):
            for out_half in range(2):
                totals = [None, None]
                for c10 in range(HALF):
                    at = ((c10 * PARTS + part) * 2 + out_half) * ROWS
                    weight = weights_ref[distance, at : at + ROWS, :].astype(jnp.float32)
                    for kind in range(2):
                        top = part * group_rows + kind * ROWS
                        term = spread[top : top + ROWS, c10 * LANES : (c10 + 1) * LANES] * weight
                        totals[kind] = term if c10 == 0 else totals[kind] + term
                for kind in range(2):
                    start = group * (4 * ROWS) + (kind * 2 + out_half) * ROWS
                    sums_ref[
                        pl.ds(pl.multiple_of(start, 8), ROWS), part * LANES : (part + 1) * LANES
                    ] = totals[kind]
    copies[6].wait()
    back = dot(inv_ref[...], sums_ref[...].astype(jnp.bfloat16))
    blocks = [
        back[:, part * LANES : (part + 1) * LANES].reshape(OWNERS, 8, LANES)
        for part in range(PARTS)
    ]
    out_ref[...] = jnp.concatenate(blocks, 1).reshape(GROUPS * 8, LANES).astype(jnp.bfloat16)


def mix_call(place, message, weights, tables):
    held = [tables["x_fwd"], tables["same"], tables["x_inv"]]
    return pl.pallas_call(
        mix_kernel,
        grid=(1,),
        in_specs=[pl.BlockSpec(memory_space=pltpu.SMEM), IN_VMEM] + [IN_HBM] * 4,
        out_specs=whole(MESSAGE),
        out_shape=pltpu.HBM(MESSAGE, jnp.bfloat16),
        scratch_shapes=[pltpu.VMEM((KX_GROUPS * 4 * ROWS, PARTS * LANES), jnp.float32)]
        + [pltpu.VMEM(table.shape, table.dtype) for table in held]
        + [pltpu.VMEM(WEIGHTS, jnp.bfloat16), pltpu.SemaphoreType.DMA((7,))],
        compiler_params=pltpu.CompilerParams(vmem_limit_bytes=VMEM_BYTES),
        name="mix_x",
    )(place, *in_vmem([message]), *map(in_hbm, held + [weights]))


WEIGHT_ROWS = HALF * PARTS * 2 * ROWS
WEIGHTS = (KX_GROUPS, WEIGHT_ROWS, LANES)


def arrange_kernel(
    own, near, far, across, select_ref, place_ref, first_ref, second_ref, shards_ref, rows_ref, done_ref, arrived, left
):
    rows = PARTS * QL * LAYERS
    arriving = [
        pltpu.make_async_copy(shard, shards_ref.at[i], arrived.at[i])
        for i, shard in enumerate((own, near, far, across))
    ]
    for copy in arriving:
        copy.start()
    leaving = []
    for distance in range(KX_GROUPS):
        arriving[distance].wait()
        split = dot(shards_ref[distance].reshape(KX_PER * rows, 2 * C * C), select_ref[...])
        columns = []
        for kx in range(KX_PER):
            block = split[kx * rows : (kx + 1) * rows]
            stacked = [block[:, out * LANES : (out + 1) * LANES] for out in range(HALF)]
            columns.append(jnp.concatenate(stacked, 0).astype(jnp.bfloat16))
        moved = lax.dot_general(
            jnp.concatenate(columns, 1),
            place_ref[...],
            (((0,), (0,)), ((), ())),
            preferred_element_type=jnp.float32,
        )
        for layer, out_ref in enumerate((first_ref, second_ref)):
            for part in range(PARTS):
                lane = (layer * PARTS + part) * LANES
                for kx in range(KX_PER):
                    for c10 in range(HALF):
                        row = kx * LANES + c10 * 8
                        start = (c10 * PARTS + part) * 2 * ROWS + kx
                        rows_ref[layer, pl.ds(start, 8, stride=KX_PER), :] = moved[
                            row : row + 8, lane : lane + LANES
                        ]
            done_ref[layer, distance] = rows_ref[layer].astype(jnp.bfloat16)
            copy = pltpu.make_async_copy(
                done_ref.at[layer, distance], out_ref.at[distance], left.at[layer, distance]
            )
            copy.start()
            leaving.append(copy)
    for copy in leaving:
        copy.wait()


def arrange_weights(shards, tables):
    held = [tables["select"], tables["place"]]
    return pl.pallas_call(
        arrange_kernel,
        grid=(1,),
        in_specs=[IN_HBM] * KX_GROUPS + [IN_VMEM] * 2,
        out_specs=[IN_HBM] * LAYERS,
        out_shape=[pltpu.HBM(WEIGHTS, jnp.bfloat16)] * LAYERS,
        scratch_shapes=[
            pltpu.VMEM((KX_GROUPS,) + shards[0].shape, shards[0].dtype),
            pltpu.VMEM((LAYERS, WEIGHT_ROWS, LANES), jnp.float32),
            pltpu.VMEM((LAYERS,) + WEIGHTS, jnp.bfloat16),
            pltpu.SemaphoreType.DMA((KX_GROUPS,)),
            pltpu.SemaphoreType.DMA((LAYERS, KX_GROUPS)),
        ],
        compiler_params=pltpu.CompilerParams(vmem_limit_bytes=VMEM_BYTES),
        name="arrange_weights",
    )(*map(in_hbm, shards), *in_vmem(held))


def swap(value, distance):
    return lax.ppermute(value, "batch", [(i, i ^ distance) for i in range(KX_GROUPS)])


def gather_weights(weights):
    own = jnp.transpose(weights, (1, 2, 0, 3))
    far = swap(own, 2)
    return [own, swap(own, 1), far, swap(far, 1)]


def exchange(message):
    grouped = message.reshape(OWNERS, PARTS * 8, LANES)
    moved = lax.all_to_all(grouped, "space", split_axis=0, concat_axis=0, tiled=True)
    return moved.reshape(MESSAGE)


def local_kernel(offset_ref, weight_ref, field_ref, out_ref, mixing_ref):
    size = C * STRIP

    @pl.when((pl.program_id(0) == 0) & (pl.program_id(1) == 0))
    def _():
        row = lax.broadcasted_iota(jnp.int32, (size, C), 0) // STRIP
        pick_out = (row == lane_index((size, C))).astype(jnp.bfloat16)
        lane = lane_index((C, size)) // STRIP
        pick_in = (lax.broadcasted_iota(jnp.int32, (C, size), 0) == lane).astype(jnp.bfloat16)
        rows = dot(pick_out, weight_ref[...]).astype(jnp.bfloat16)
        full = dot(rows, pick_in)
        same = lax.rem(lax.broadcasted_iota(jnp.int32, (size, size), 0), STRIP) == lax.rem(
            lane_index((size, size)), STRIP
        )
        mixing_ref[...] = jnp.where(same, full, 0.0).astype(jnp.bfloat16)

    for first in range(0, LOCAL_ROWS, STRIP):
        mixed = dot(mixing_ref[...], field_ref[:, :, 0, first : first + STRIP].reshape(size, ZT))
        for half in range(2):
            for c10 in range(HALF):
                channel = half * HALF + c10
                rows = mixed[channel * STRIP : (channel + 1) * STRIP] + 0.5 * offset_ref[channel]
                out_ref[half, c10, 0, first : first + STRIP] = rows.astype(jnp.bfloat16)


def local_term(current, weight, offset):
    spec = pl.BlockSpec((2, HALF, 1, LOCAL_ROWS, ZT), lambda p, y: (0, 0, p, y, 0))
    return pl.pallas_call(
        local_kernel,
        grid=(PLANES, Y // LOCAL_ROWS),
        in_specs=[pl.BlockSpec(memory_space=pltpu.SMEM), whole((C, C)), spec],
        out_specs=spec,
        out_shape=pltpu.HBM(FIELD, jnp.bfloat16),
        scratch_shapes=[pltpu.VMEM((C * STRIP, C * STRIP), jnp.bfloat16)],
        compiler_params=pltpu.CompilerParams(vmem_limit_bytes=VMEM_BYTES),
        name="local_mixing",
    )(offset, (0.5 * weight).T, in_hbm(current))


def after(value, *others):
    return lax.optimization_barrier((value,) + others)[0]


def body(field, spectral_weight, local_weight, bias):
    tables = {name: jnp.asarray(table) for name, table in build_tables().items()}
    place = lax.axis_index("batch").astype(jnp.int32).reshape(1)
    field = field.reshape(FIELD)
    own, near, far, across = gather_weights(spectral_weight)
    message = forward_call(field, tables)
    weights = arrange_weights([after(own, message), near, far, across], tables)
    back = mix_call(place, exchange(message), weights[0], tables)
    local = local_term(field, after(local_weight[0], back), bias[0])
    current, message = turn_call(exchange(back), local, tables)
    local = local_term(current, local_weight[1], bias[1])
    back = mix_call(place, after(exchange(message), local), weights[1], tables)
    return inverse_call(exchange(back), local, tables).reshape(1, C, PLANES, Y, ZT)


def solution(mesh):
    placed = (P("batch", None, "space", None, None), P(None, "batch", "space", None), P(), P())
    return jax.shard_map(
        body,
        mesh=mesh,
        in_specs=placed,
        out_specs=P("batch", None, "space", None, None),
        check_vma=False,
    )
```

```python
import math

import jax
import jax.numpy as jnp
import numpy as np
from jax import lax
from jax.experimental import pallas as pl
from jax.experimental.pallas import tpu as pltpu
from jax.sharding import PartitionSpec as P

X = 128
Y = 128
VERTICAL_POINTS = 32
EPOCH_COUNT = 16
ZT = VERTICAL_POINTS * EPOCH_COUNT
C = 20
MX = 24
MY = 24
MZ = 12
MT = 8
LAYERS = 2

QL = 12
QH = MZ * MT // QL
GROUPS = MY * QH
PARTS = 3
HALF = C // 2
LANES = 128
PLANES = 2
OWNERS = X // PLANES
KX_GROUPS = 4
KX_PER = MX // KX_GROUPS
ROWS = 2 * 2 * KX_PER
PAIRS = 2
STEPS = HALF // PAIRS
STRIP = 16
LOCAL_ROWS = 64
VMEM_BYTES = 48 << 20

ERF_COEFFICIENTS = (
    7.97884216e-01,
    3.63342831e-02,
    -3.31296180e-05,
    -5.52402773e-05,
    3.96912621e-06,
    -1.33447465e-07,
    1.80564042e-09,
)
HALVED_COEFFICIENTS = tuple(2.0 * 4.0**i * c for i, c in enumerate(ERF_COEFFICIENTS))


def line_table(length, kept_count):
    half = kept_count // 2
    frequency = np.concatenate([np.arange(half), np.arange(length - half, length)])
    angles = 2.0 * math.pi / length * (np.arange(length)[:, None] * frequency[None, :] % length)
    cosine = np.cos(angles) / math.sqrt(length)
    sine = np.sin(angles) / math.sqrt(length)
    forward = np.stack([np.stack([cosine, -sine], 1), np.stack([sine, cosine], 1)], 1)
    inverse = np.stack([np.stack([cosine.T, sine.T], -1), np.stack([-sine.T, cosine.T], -1)], 1)
    return forward, inverse


def depth_table():
    half = MZ // 2
    vertical = np.concatenate([np.arange(half), np.arange(VERTICAL_POINTS - half, VERTICAL_POINTS)])
    clock = np.arange(MT)
    cells = np.arange(ZT)
    turns = (
        (cells // EPOCH_COUNT)[:, None, None] * vertical[None, :, None] * EPOCH_COUNT
        + (cells % EPOCH_COUNT)[:, None, None] * clock[None, None, :] * VERTICAL_POINTS
    ) % ZT
    angles = 2.0 * math.pi / ZT * turns.reshape(ZT, MZ * MT)
    cosine = np.cos(angles) / math.sqrt(ZT)
    sine = np.sin(angles) / math.sqrt(ZT)
    doubling = np.broadcast_to(np.where(clock == 0, 1.0, 2.0)[None, :], (MZ, MT)).reshape(-1)
    kept = MZ * MT
    forward = np.zeros((ZT, 2 * LANES))
    forward[:, :kept] = cosine
    forward[:, LANES : LANES + kept] = -sine
    inverse = np.zeros((2 * LANES, ZT))
    inverse[:kept] = cosine.T * doubling[:, None]
    inverse[LANES : LANES + kept] = -sine.T * doubling[:, None]
    return forward, 0.5 * inverse


def build_tables():
    zt_forward, zt_inverse = depth_table()
    y_forward, y_inverse = line_table(Y, MY)
    x_forward, x_inverse = line_table(X, MX)
    eye = np.eye(2)
    y_fwd = np.einsum("yrjm,ab,uv->maujbrvy", y_forward, eye, eye)
    y_fwd = y_fwd.reshape(MY * 8, 4 * PLANES * Y)
    y_inv = np.einsum("mryj,ab,uv->ajuymbvr", y_inverse, eye, eye)
    y_inv = y_inv.reshape(4 * PLANES * Y, MY * 8)
    x_split = x_forward.reshape(OWNERS, PLANES, 2, 2, KX_GROUPS, KX_PER)
    x_re, x_im = x_split[:, :, :, 0], x_split[:, :, :, 1]
    parts = np.stack([np.stack([x_re, -x_im]), np.stack([x_im, x_re])])
    x_fwd = np.einsum("stiurgm,ab->gsatmibur", parts, eye)
    x_fwd = x_fwd.reshape(KX_GROUPS * 2 * ROWS, OWNERS * 8)
    x_split = x_inverse.reshape(KX_GROUPS, KX_PER, 2, OWNERS, PLANES, 2)
    x_inv = np.einsum("gmsiuj,ab,c,t->iaujgsbctm", x_split, eye, np.ones(2), np.ones(2))
    x_inv = x_inv.reshape(OWNERS * 8, KX_GROUPS * 4 * ROWS)
    same = np.tile(np.eye(QL), (HALF, HALF))
    same = np.pad(same, (0, LANES - HALF * QL))
    select = np.einsum("ci,hu,ta,rs,op->rtchopiuas", np.eye(HALF), eye, eye, eye, np.eye(HALF))
    select = select.reshape(2 * C * C, HALF, 8 * HALF)
    select = np.pad(select, ((0, 0), (0, 0), (0, LANES - 8 * HALF))).reshape(2 * C * C, -1)
    place = np.einsum(
        "or,pa,qb,lm->opqlmarb", np.eye(HALF), np.eye(PARTS), np.eye(QL), np.eye(LAYERS)
    )
    place = place.reshape(HALF * PARTS * QL * LAYERS, LAYERS * PARTS, HALF * QL)
    place = np.pad(place, ((0, 0), (0, 0), (0, LANES - HALF * QL)))
    place = place.reshape(HALF * PARTS * QL * LAYERS, -1)
    held = {
        "zt_fwd": zt_forward,
        "zt_inv": zt_inverse,
        "y_fwd": y_fwd,
        "y_inv": y_inv,
        "x_fwd": x_fwd,
        "x_inv": x_inv,
        "same": same,
        "select": select,
        "place": place,
    }
    return {name: table.astype(np.float32).astype(jnp.bfloat16) for name, table in held.items()}


def lane_index(shape):
    return lax.broadcasted_iota(jnp.int32, shape, len(shape) - 1)


def dot(left, right):
    return jnp.dot(left, right, preferred_element_type=jnp.float32)


def forward_step(step, block, zt_table, y_table, modes_ref):
    zt_fwd = zt_table[...]
    columns = []
    for pair in range(PAIRS):
        rows = []
        for half in range(2):
            z = dot(block(half, pair), zt_fwd).astype(jnp.bfloat16)
            rows += [z[:, :LANES], z[:, LANES:]]
        columns.append(jnp.concatenate(rows, 0))
    modes = dot(y_table[...], jnp.concatenate(columns, 1))
    for pair in range(PAIRS):
        modes_ref[step * PAIRS + pair] = modes[:, pair * LANES : (pair + 1) * LANES]


def group_masks():
    lane = lane_index((MY * 8, LANES))
    return [(lane >= g * QL) & (lane < g * QL + QL) for g in range(HALF)]


OFFSETS = range(1 - QH, HALF)


def pack_modes(modes_ref, turned_ref):
    masks = group_masks()
    for place, offset in enumerate(OFFSETS):
        value = jnp.zeros((MY * 8, LANES), jnp.float32)
        for qh in range(QH):
            if 0 <= qh + offset < HALF:
                value = jnp.where(masks[qh], modes_ref[qh + offset], value)
        turned_ref[place] = pltpu.roll(value, offset * QL % LANES, 1)
    strips = []
    for qh in range(QH):
        value = jnp.zeros((MY * 8, LANES), jnp.float32)
        for channel in range(HALF):
            value = jnp.where(masks[channel], turned_ref[channel - qh + QH - 1], value)
        strips.append(value.reshape(MY, 1, 8, LANES))
    return jnp.concatenate(strips, 1).reshape(GROUPS * 8, LANES).astype(jnp.bfloat16)


def unpack_modes(message_ref, modes_ref, turned_ref):
    masks = group_masks()
    message = message_ref[...].astype(jnp.float32).reshape(MY, QH, 8, LANES)
    strips = [message[:, qh].reshape(MY * 8, LANES) for qh in range(QH)]
    for place, offset in enumerate(OFFSETS):
        value = jnp.zeros((MY * 8, LANES), jnp.float32)
        for qh in range(QH):
            if 0 <= qh + offset < HALF:
                value = jnp.where(masks[qh + offset], strips[qh], value)
        turned_ref[place] = pltpu.roll(value, -offset * QL % LANES, 1)
    for channel in range(HALF):
        value = jnp.zeros((MY * 8, LANES), jnp.float32)
        for qh in range(QH):
            value = jnp.where(masks[qh], turned_ref[channel - qh + QH - 1], value)
        modes_ref[channel] = value.astype(jnp.bfloat16)


def forward_kernel(field_ref, zt_ref, y_ref, out_ref, modes_ref, turned_ref):
    step = pl.program_id(0)

    def block(half, pair):
        return field_ref[half, pair].reshape(PLANES * Y, ZT)

    forward_step(step, block, zt_ref, y_ref, modes_ref)

    @pl.when(step == STEPS - 1)
    def _():
        out_ref[...] = pack_modes(modes_ref, turned_ref)


IN_VMEM = pl.BlockSpec(memory_space=pltpu.VMEM)
IN_HBM = pl.BlockSpec(memory_space=pltpu.HBM)


def in_vmem(arrays):
    return [pltpu.with_memory_space_constraint(array, pltpu.VMEM) for array in arrays]


def in_hbm(array):
    return pltpu.with_memory_space_constraint(array, pltpu.HBM)


def whole(shape):
    return pl.BlockSpec(shape, lambda *_: (0,) * len(shape), pipeline_mode=pl.Buffered(1))


def field_spec():
    return pl.BlockSpec((2, PAIRS, PLANES, Y, ZT), lambda s: (0, s, 0, 0, 0))


MESSAGE = (GROUPS * 8, LANES)
SENT_MODES = pltpu.VMEM((HALF, MY * 8, LANES), jnp.float32)
GOT_MODES = pltpu.VMEM((HALF, MY * 8, LANES), jnp.bfloat16)
TURNED = pltpu.VMEM((len(OFFSETS), MY * 8, LANES), jnp.float32)


def forward_call(field, tables):
    return pl.pallas_call(
        forward_kernel,
        grid=(STEPS,),
        in_specs=[field_spec()] + [whole(tables[name].shape) for name in ("zt_fwd", "y_fwd")],
        out_specs=whole(MESSAGE),
        out_shape=pltpu.HBM(MESSAGE, jnp.bfloat16),
        scratch_shapes=[SENT_MODES, TURNED],
        compiler_params=pltpu.CompilerParams(vmem_limit_bytes=VMEM_BYTES),
        name="forward_zt_y",
    )(in_hbm(field), in_hbm(tables["zt_fwd"]), in_hbm(tables["y_fwd"]))


def gelu(h):
    s = h * h
    p = jnp.float32(HALVED_COEFFICIENTS[-1])
    for coefficient in HALVED_COEFFICIENTS[-2::-1]:
        p = p * s + jnp.float32(coefficient)
    return h + h * jnp.tanh(h * p)


def inverse_step(step, modes_ref, local_ref, y_table, zt_table, out_ref):
    columns = [modes_ref[step * PAIRS + pair] for pair in range(PAIRS)]
    back = dot(y_table[...], jnp.concatenate(columns, 1)).astype(jnp.bfloat16)
    zt_inv = zt_table[...]
    span = PLANES * Y
    results = {}
    for pair in range(PAIRS):
        own = back[:, pair * LANES : (pair + 1) * LANES]
        for half in range(2):
            at = 2 * half * span
            rows = jnp.concatenate([own[at : at + span], own[at + span : at + 2 * span]], 1)
            total = dot(rows, zt_inv) + local_ref[half, pair].reshape(span, ZT)
            result = gelu(total).astype(jnp.bfloat16)
            out_ref[half, pair] = result.reshape(PLANES, Y, ZT)
            results[half, pair] = result
    return results


def inverse_kernel(local_ref, message_ref, y_ref, zt_ref, out_ref, modes_ref, turned_ref):
    step = pl.program_id(0)

    @pl.when(step == 0)
    def _():
        unpack_modes(message_ref, modes_ref, turned_ref)

    inverse_step(step, modes_ref, local_ref, y_ref, zt_ref, out_ref)


FIELD = (2, HALF, PLANES, Y, ZT)


def inverse_call(message, local, tables):
    held = [message, tables["y_inv"], tables["zt_inv"]]
    return pl.pallas_call(
        inverse_kernel,
        grid=(STEPS,),
        in_specs=[field_spec()] + [IN_VMEM] * 3,
        out_specs=field_spec(),
        out_shape=pltpu.HBM(FIELD, jnp.bfloat16),
        scratch_shapes=[GOT_MODES, TURNED],
        compiler_params=pltpu.CompilerParams(vmem_limit_bytes=VMEM_BYTES),
        name="inverse_zt_y",
    )(in_hbm(local), *in_vmem(held))


def turn_kernel(
    local_ref, message_ref, y_inv, zt_inv, zt_fwd, y_fwd, out_ref, send_ref, modes_ref, next_ref, turned_ref
):
    step = pl.program_id(0)

    @pl.when(step == 0)
    def _():
        unpack_modes(message_ref, modes_ref, turned_ref)

    results = inverse_step(step, modes_ref, local_ref, y_inv, zt_inv, out_ref)

    def block(half, pair):
        return results[half, pair]

    forward_step(step, block, zt_fwd, y_fwd, next_ref)

    @pl.when(step == STEPS - 1)
    def _():
        send_ref[...] = pack_modes(next_ref, turned_ref)


def turn_call(message, local, tables):
    held = [message] + [tables[name] for name in ("y_inv", "zt_inv", "zt_fwd", "y_fwd")]
    return pl.pallas_call(
        turn_kernel,
        grid=(STEPS,),
        in_specs=[field_spec()] + [IN_VMEM] * len(held),
        out_specs=[field_spec(), whole(MESSAGE)],
        out_shape=[
            pltpu.HBM(FIELD, jnp.bfloat16),
            pltpu.HBM(MESSAGE, jnp.bfloat16),
        ],
        scratch_shapes=[GOT_MODES, SENT_MODES, TURNED],
        compiler_params=pltpu.CompilerParams(vmem_limit_bytes=VMEM_BYTES),
        name="inverse_then_forward",
    )(in_hbm(local), *in_vmem(held))


def mix_kernel(
    place_ref, message_ref, x_hbm, same_hbm, inv_hbm, weights_hbm, out_ref, sums_ref, x_table,
    same_ref, inv_ref, weights_ref, arrived
):
    pairs = [(x_hbm, x_table), (same_hbm, same_ref)]
    pairs += [(weights_hbm.at[i], weights_ref.at[i]) for i in range(KX_GROUPS)]
    pairs.append((inv_hbm, inv_ref))
    copies = [
        pltpu.make_async_copy(source, target, arrived.at[i])
        for i, (source, target) in enumerate(pairs)
    ]
    for copy in copies:
        copy.start()
    span = OWNERS * 8
    message = message_ref[...].astype(jnp.float32).reshape(OWNERS, PARTS * 8, LANES)
    pieces = [
        message[:, part * 8 : part * 8 + 8].reshape(span, LANES).astype(jnp.bfloat16)
        for part in range(PARTS)
    ]
    pieces = jnp.concatenate(pieces, 1)
    copies[0].wait()
    copies[1].wait()
    same = same_ref[...].astype(jnp.float32)
    row = lax.broadcasted_iota(jnp.int32, same.shape, 0)
    spread_table = [
        jnp.where((row >= c10 * QL) & (row < c10 * QL + QL), same, 0.0) for c10 in range(HALF)
    ]
    spread_table = jnp.concatenate(spread_table, 1).astype(jnp.bfloat16)
    group_rows = 2 * ROWS
    for distance in range(KX_GROUPS):
        group = place_ref[0] ^ distance
        table = x_table[pl.ds(pl.multiple_of(group * group_rows, group_rows), group_rows), :]
        modes = dot(table, pieces).astype(jnp.bfloat16)
        rows = [modes[:, part * LANES : (part + 1) * LANES] for part in range(PARTS)]
        spread = dot(jnp.concatenate(rows, 0), spread_table)
        copies[2 + distance].wait()
        for part in range(PARTS):
            for out_half in range(2):
                totals = [None, None]
                for c10 in range(HALF):
                    at = ((c10 * PARTS + part) * 2 + out_half) * ROWS
                    weight = weights_ref[distance, at : at + ROWS, :].astype(jnp.float32)
                    for kind in range(2):
                        top = part * group_rows + kind * ROWS
                        term = spread[top : top + ROWS, c10 * LANES : (c10 + 1) * LANES] * weight
                        totals[kind] = term if c10 == 0 else totals[kind] + term
                for kind in range(2):
                    start = group * (4 * ROWS) + (kind * 2 + out_half) * ROWS
                    sums_ref[
                        pl.ds(pl.multiple_of(start, 8), ROWS), part * LANES : (part + 1) * LANES
                    ] = totals[kind]
    copies[6].wait()
    back = dot(inv_ref[...], sums_ref[...].astype(jnp.bfloat16))
    blocks = [
        back[:, part * LANES : (part + 1) * LANES].reshape(OWNERS, 8, LANES)
        for part in range(PARTS)
    ]
    out_ref[...] = jnp.concatenate(blocks, 1).reshape(GROUPS * 8, LANES).astype(jnp.bfloat16)


def mix_call(place, message, weights, tables, pin):
    held = [tables["x_fwd"], tables["same"], tables["x_inv"]]
    return pl.pallas_call(
        mix_kernel,
        grid=(1,),
        in_specs=[pl.BlockSpec(memory_space=pltpu.SMEM), IN_VMEM] + [pl.BlockSpec(memory_space=pl.ANY)] * 4,
        out_specs=whole(MESSAGE),
        out_shape=pltpu.HBM(MESSAGE, jnp.bfloat16),
        scratch_shapes=[pltpu.VMEM((KX_GROUPS * 4 * ROWS, PARTS * LANES), jnp.float32)]
        + [pltpu.VMEM(table.shape, table.dtype) for table in held]
        + [pltpu.VMEM(WEIGHTS, jnp.bfloat16), pltpu.SemaphoreType.DMA((7,))],
        compiler_params=pltpu.CompilerParams(vmem_limit_bytes=VMEM_BYTES),
        name="mix_x",
    )(place, *in_vmem([message]), *pin(held + [weights]))


WEIGHT_ROWS = HALF * PARTS * 2 * ROWS
WEIGHTS = (KX_GROUPS, WEIGHT_ROWS, LANES)


def arrange_kernel(
    own, near, far, across, select_ref, place_ref, first_ref, second_ref, shards_ref, rows_ref, done_ref, arrived, left
):
    rows = PARTS * QL * LAYERS
    arriving = [
        pltpu.make_async_copy(shard, shards_ref.at[i], arrived.at[i])
        for i, shard in enumerate((own, near, far, across))
    ]
    for copy in arriving:
        copy.start()
    leaving = []
    for distance in range(KX_GROUPS):
        arriving[distance].wait()
        split = dot(shards_ref[distance].reshape(KX_PER * rows, 2 * C * C), select_ref[...])
        columns = []
        for kx in range(KX_PER):
            block = split[kx * rows : (kx + 1) * rows]
            stacked = [block[:, out * LANES : (out + 1) * LANES] for out in range(HALF)]
            columns.append(jnp.concatenate(stacked, 0).astype(jnp.bfloat16))
        moved = lax.dot_general(
            jnp.concatenate(columns, 1),
            place_ref[...],
            (((0,), (0,)), ((), ())),
            preferred_element_type=jnp.float32,
        )
        for layer, out_ref in enumerate((first_ref, second_ref)):
            for part in range(PARTS):
                lane = (layer * PARTS + part) * LANES
                for kx in range(KX_PER):
                    for c10 in range(HALF):
                        row = kx * LANES + c10 * 8
                        start = (c10 * PARTS + part) * 2 * ROWS + kx
                        rows_ref[layer, pl.ds(start, 8, stride=KX_PER), :] = moved[
                            row : row + 8, lane : lane + LANES
                        ]
            done_ref[layer, distance] = rows_ref[layer].astype(jnp.bfloat16)
            copy = pltpu.make_async_copy(
                done_ref.at[layer, distance], out_ref.at[distance], left.at[layer, distance]
            )
            copy.start()
            leaving.append(copy)
    for copy in leaving:
        copy.wait()


def arrange_weights(shards, tables):
    held = [tables["select"], tables["place"]]
    return pl.pallas_call(
        arrange_kernel,
        grid=(1,),
        in_specs=[IN_HBM] * KX_GROUPS + [IN_VMEM] * 2,
        out_specs=[IN_HBM] * LAYERS,
        out_shape=[pltpu.HBM(WEIGHTS, jnp.bfloat16)] * LAYERS,
        scratch_shapes=[
            pltpu.VMEM((KX_GROUPS,) + shards[0].shape, shards[0].dtype),
            pltpu.VMEM((LAYERS, WEIGHT_ROWS, LANES), jnp.float32),
            pltpu.VMEM((LAYERS,) + WEIGHTS, jnp.bfloat16),
            pltpu.SemaphoreType.DMA((KX_GROUPS,)),
            pltpu.SemaphoreType.DMA((LAYERS, KX_GROUPS)),
        ],
        compiler_params=pltpu.CompilerParams(vmem_limit_bytes=VMEM_BYTES),
        name="arrange_weights",
    )(*map(in_hbm, shards), *in_vmem(held))


def swap(value, distance):
    return lax.ppermute(value, "batch", [(i, i ^ distance) for i in range(KX_GROUPS)])


def gather_weights(weights):
    own = jnp.transpose(weights, (1, 2, 0, 3))
    far = swap(own, 2)
    return [own, swap(own, 1), far, swap(far, 1)]


def exchange(message):
    grouped = message.reshape(OWNERS, PARTS * 8, LANES)
    moved = lax.all_to_all(grouped, "space", split_axis=0, concat_axis=0, tiled=True)
    return moved.reshape(MESSAGE)


def local_kernel(offset_ref, weight_ref, field_ref, out_ref, mixing_ref):
    size = C * STRIP

    @pl.when((pl.program_id(0) == 0) & (pl.program_id(1) == 0))
    def _():
        row = lax.broadcasted_iota(jnp.int32, (size, C), 0) // STRIP
        pick_out = (row == lane_index((size, C))).astype(jnp.bfloat16)
        lane = lane_index((C, size)) // STRIP
        pick_in = (lax.broadcasted_iota(jnp.int32, (C, size), 0) == lane).astype(jnp.bfloat16)
        rows = dot(pick_out, weight_ref[...]).astype(jnp.bfloat16)
        full = dot(rows, pick_in)
        same = lax.rem(lax.broadcasted_iota(jnp.int32, (size, size), 0), STRIP) == lax.rem(
            lane_index((size, size)), STRIP
        )
        mixing_ref[...] = jnp.where(same, full, 0.0).astype(jnp.bfloat16)

    for first in range(0, LOCAL_ROWS, STRIP):
        mixed = dot(mixing_ref[...], field_ref[:, :, 0, first : first + STRIP].reshape(size, ZT))
        for half in range(2):
            for c10 in range(HALF):
                channel = half * HALF + c10
                rows = mixed[channel * STRIP : (channel + 1) * STRIP] + 0.5 * offset_ref[channel]
                out_ref[half, c10, 0, first : first + STRIP] = rows.astype(jnp.bfloat16)


def local_term(current, weight, offset):
    spec = pl.BlockSpec((2, HALF, 1, LOCAL_ROWS, ZT), lambda p, y: (0, 0, p, y, 0))
    return pl.pallas_call(
        local_kernel,
        grid=(PLANES, Y // LOCAL_ROWS),
        in_specs=[pl.BlockSpec(memory_space=pltpu.SMEM), whole((C, C)), spec],
        out_specs=spec,
        out_shape=pltpu.HBM(FIELD, jnp.bfloat16),
        scratch_shapes=[pltpu.VMEM((C * STRIP, C * STRIP), jnp.bfloat16)],
        compiler_params=pltpu.CompilerParams(vmem_limit_bytes=VMEM_BYTES),
        name="local_mixing",
    )(offset, (0.5 * weight).T, in_hbm(current))


def after(value, *others):
    return lax.optimization_barrier((value,) + others)[0]


def body(field, spectral_weight, local_weight, bias):
    tables = {name: jnp.asarray(table) for name, table in build_tables().items()}
    place = lax.axis_index("batch").astype(jnp.int32).reshape(1)
    field = field.reshape(FIELD)
    own, near, far, across = gather_weights(spectral_weight)
    message = forward_call(field, tables)
    message = after(message, near)
    weights = arrange_weights([after(own, message), near, far, across], tables)
    back = mix_call(place, exchange(message), weights[0], tables, lambda arrays: map(in_hbm, arrays))
    local = local_term(field, after(local_weight[0], back), bias[0])
    current, message = turn_call(exchange(back), local, tables)
    local = local_term(current, local_weight[1], bias[1])
    back = mix_call(place, after(exchange(message), local), weights[1], tables, in_vmem)
    return inverse_call(exchange(back), local, tables).reshape(1, C, PLANES, Y, ZT)


def solution(mesh):
    placed = (P("batch", None, "space", None, None), P(None, "batch", "space", None), P(), P())
    return jax.shard_map(
        body,
        mesh=mesh,
        in_specs=placed,
        out_specs=P("batch", None, "space", None, None),
        check_vma=False,
    )
```
